32 devices in a mesh: parts: 2 (over y), blk: 16 (over z, x, core).
Axes of the slice: x: 2, y: 2, z: 4, core: 2. Of those that a mesh axis runs over, the one named last changes fastest.
Arguments:
- series: bfloat16 [16, 192, 11264], P(None, None, 'blk'), may hold values from -24 to 24
- subject_ids: int32 [16], P('parts'), parts along dimension 0, may hold values from 0 to 15
- net_labels: int32 [16], replicated, may hold values from 0 to 6
Outputs:
- connectome: float32 [22528, 11264], P(('parts', 'blk')), parts along dimension 0
The draws below stay inside these ranges and needn't reach their ends.
There are 2 independent parts, one for each index of `parts`. The reference program is written for one: setup_inputs(seed, part) draws one part's arguments, and reference() takes and returns one part's arrays. A program takes and returns all parts, laid end to end along the dimension named above; an argument that names none is the same for every part. Nothing has to cross between parts.
Inputs may be any that keep to these rules, and one draw needn't show every extreme that they name: `subject_ids`: indices into the pool; a subject may repeat.
All inputs are finite; a program needn't handle non-finite values.
Results may differ from the reference program's by a relative error of at most 0.00072.
Values may be sent and summed in bfloat16 or wider, within the bound.
A program may use at most 384 MiB of HBM per device.

```python
import math
import jax
import jax.numpy as jnp
import numpy as np
from jax import lax

BLOCK = 704
NBLOCK = 16
NET = 7
SUBJ = 8
POOL = 16
FRAMES = 192
G = 11264


def draw_series(key, part):
    keys = jax.random.split(key, 4)
    own = jax.random.truncated_normal(keys[0], -4.0, 4.0, (POOL, FRAMES, NBLOCK), jnp.float32)
    common = jax.random.truncated_normal(keys[1], -4.0, 4.0, (POOL, FRAMES, 1), jnp.float32)
    latent = jnp.repeat(own + 0.7 * common, BLOCK, axis=2)
    loading = jax.random.uniform(keys[2], (POOL, 1, G), jnp.float32, 0.8, 2.5)
    noise = jax.random.truncated_normal(keys[3], -4.0, 4.0, (POOL, FRAMES, G), jnp.float32)
    values = loading * latent + noise
    return values.astype(jnp.bfloat16)


def with_ends(values, key, least, largest):
    extent = values.shape
    place = [jax.random.randint(jax.random.fold_in(key, axis), (), 0, extent[axis]) for axis in range(len(extent))]
    values = values.at[tuple(place)].set(least)
    longest = extent.index(max(extent))
    place[longest] = (place[longest] + 1) % extent[longest]
    return values.at[tuple(place)].set(largest)


def rank_bounds(count, lean):
    portions = [(1 << 20) // math.isqrt(standing ** lean) + 1 for standing in range(1, count + 1)]
    scale = 1 + sum(portions) // (1 << 30)
    return np.cumsum(np.array([max(1, weight // scale) for weight in portions]))


def skewed_ids(stream_key, shape, count, skew):
    grid = rank_bounds(count, skew)
    pick = jax.random.randint(jax.random.fold_in(stream_key, 1), shape, 0, int(grid[count - 1]))
    rank = jnp.searchsorted(jnp.asarray(grid, jnp.int32), pick, side="right")
    return jax.random.permutation(jax.random.fold_in(stream_key, 2), count)[rank].astype(jnp.int32)


def setup_inputs(seed: int = 0, part: int = 0) -> dict:
    streams_of = jax.random.split(jax.random.key(seed), 4)
    part_keys = jax.random.split(jax.random.fold_in(streams_of[3], part), 4)
    return {
        "series": draw_series(jax.random.fold_in(streams_of[3], 71), part),
        "subject_ids": with_ends(jax.random.randint(part_keys[1], (SUBJ,), 0, POOL), jax.random.fold_in(part_keys[1], 1), 0, POOL - 1).astype(jnp.int32),
        "net_labels": with_ends(skewed_ids(streams_of[2], (NBLOCK,), NET, 2), jax.random.fold_in(streams_of[2], 3), 0, NET - 1).astype(jnp.int32),
    }


def fisher_value(corr):
    clipped = jnp.clip(corr, -0.999, 0.999)
    return 0.5 * jnp.log((1.0 + clipped) / (1.0 - clipped))

def reference(series, subject_ids, net_labels):
    chosen = series[subject_ids].astype(jnp.float32)
    center = chosen - lax.optimization_barrier(jnp.mean(chosen, axis=1, keepdims=True))
    spread = lax.optimization_barrier(jnp.mean(center * center, axis=1, keepdims=True))
    normalized = (center / jnp.sqrt(spread + 1e-05)).astype(jnp.bfloat16)
    row_labels = jnp.repeat(net_labels, BLOCK)
    blocks = normalized.reshape(SUBJ, FRAMES, NBLOCK, BLOCK).transpose(2, 0, 1, 3)

    def one_block(inputs):
        block_rows, label = inputs
        total = jnp.zeros((BLOCK, G), jnp.float32)
        for subject in range(SUBJ):
            corr = jnp.dot(block_rows[subject].T, normalized[subject], preferred_element_type=jnp.float32) / FRAMES
            total = total + fisher_value(corr)
        return jnp.where(label == row_labels[None, :], total, jnp.zeros_like(total))
    result = lax.map(one_block, (blocks, net_labels))
    return result.reshape(G, G)
```

```python
import functools
import math

import jax
import jax.numpy as jnp
from jax import lax
from jax.experimental import pallas as pl
from jax.experimental.pallas import tpu as pltpu
from jax.sharding import PartitionSpec as P

LIMIT = 0.999
LANES = 128
HALF = LANES // 2
FORMS = [(4, 2), (5, 2), (6, 2), (7, 1), (8, 0)]


def normalize(chosen):
    values = chosen.astype(jnp.float32)
    center = values - jnp.mean(values, axis=1, keepdims=True)
    spread = jnp.mean(center * center, axis=1, keepdims=True)
    return (center / jnp.sqrt(spread + 1e-05)).astype(jnp.bfloat16)


def fisher_sum(left, right):
    frames = left.shape[1]
    total = jnp.zeros((left.shape[2], right.shape[2]), jnp.float32)
    for subject in range(left.shape[0]):
        corr = (
            lax.dot_general(
                left[subject],
                right[subject],
                (((0,), (0,)), ((), ())),
                preferred_element_type=jnp.float32,
            )
            / frames
        )
        clipped = jnp.clip(corr, -LIMIT, LIMIT)
        total = total + 0.5 * jnp.log((1.0 + clipped) / (1.0 - clipped))
    return total


def plain(series, subject_ids, net_labels):
    normalized = normalize(jnp.take(series, subject_ids, axis=0))
    rows = normalized.shape[2]
    index = lax.axis_index("blk")
    count = lax.axis_size("blk")
    row_labels = jnp.repeat(net_labels, count * rows // net_labels.shape[0])
    own_labels = lax.dynamic_slice_in_dim(row_labels, index * rows, rows)
    gathered = lax.all_gather(normalized, "blk", axis=2, tiled=True)
    same = own_labels[:, None] == row_labels[None, :]
    return jnp.where(same, fisher_sum(normalized, gathered), 0.0)


def plan_kernel(pool, mine_ref, theirs_ref, first_ref, list_ref, slot_ref, form_ref, where_ref):
    subjects = mine_ref.shape[0]
    one, zero = jnp.int32(1), jnp.int32(0)

    def members(ref):
        bits = zero
        for s in range(subjects):
            bits = bits | (one << ref[s])
        return [(bits >> p) & 1 for p in range(pool)]

    mine, theirs = members(mine_ref), members(theirs_ref)
    own, other = sum(mine), sum(theirs)
    both = sum(a * b for a, b in zip(mine, theirs))
    form = jnp.int32(len(FORMS) - 1)
    held = jnp.int32(FORMS[-1][0])
    for index in reversed(range(len(FORMS) - 1)):
        carried, passed = FORMS[index]
        lack, give = jnp.maximum(own - carried, 0), jnp.maximum(other - carried, 0)
        fits = jnp.logical_and(jnp.maximum(lack, give) <= passed, lack + give <= both)
        form = jnp.where(fits, index, form)
        held = jnp.where(fits, carried, held)
    form_ref[0] = form
    lack, give = jnp.maximum(own - held, 0), jnp.maximum(other - held, 0)
    first = first_ref[0] == 0
    give_from = jnp.where(first, 0, lack)
    lack_from = jnp.where(first, give, 0)
    for s in range(list_ref.shape[0]):
        list_ref[s] = mine_ref[0]
    rank, plain_at = zero, give
    for p in range(pool):
        common = mine[p] * theirs[p]
        gives = jnp.logical_and(rank >= give_from, rank < give_from + give)
        gives = jnp.logical_and(gives, common == 1)
        lacks = jnp.logical_and(rank >= lack_from, rank < lack_from + lack)
        lacks = jnp.logical_and(lacks, common == 1)
        at = jnp.where(gives, rank - give_from, jnp.where(lacks, held + rank - lack_from, plain_at))
        kept = jnp.logical_and(mine[p] == 1, jnp.logical_not(jnp.logical_or(gives, lacks)))
        plain_at = plain_at + kept.astype(jnp.int32)
        rank = rank + common
        where_ref[p] = at
        list_ref[jnp.where(mine[p] == 1, at, subjects)] = jnp.int32(p)
    for s in range(subjects):
        slot_ref[s] = where_ref[mine_ref[s]]


def distinct(pool, mine, theirs, part):
    subjects = mine.shape[0]
    sizes = [subjects + 1, subjects, 1]
    return pl.pallas_call(
        functools.partial(plan_kernel, pool),
        out_shape=[jax.ShapeDtypeStruct((size,), jnp.int32) for size in sizes],
        in_specs=[pl.BlockSpec(memory_space=pltpu.SMEM)] * 3,
        out_specs=[pl.BlockSpec(memory_space=pltpu.SMEM)] * 3,
        scratch_shapes=[pltpu.SMEM((pool,), jnp.int32)],
        name="plan",
    )(mine, theirs, part)


def normalize_kernel(ids_ref, me_ref, series_ref, out_ref, turned_ref):
    values = series_ref[0].astype(jnp.float32)
    frames = values.shape[0]
    center = values - jnp.sum(values, axis=0, keepdims=True) / frames
    spread = jnp.sum(center * center, axis=0, keepdims=True) / frames
    result = center / jnp.sqrt(spread + 1e-05)
    packed = result.astype(jnp.bfloat16)
    turned_ref[0] = packed.T
    width = packed.shape[1]
    tiles, top = width // LANES, frames // 2

    def pack(first, edge, upper, lower):
        for t in range(tiles):
            start = first + t * LANES
            out_ref[0, 0, t * frames : (t + 1) * frames, :] = packed[:, start : start + LANES]
        ends = {upper: packed[:top, edge : edge + HALF], lower: packed[top:, edge : edge + HALF]}
        out_ref[0, 0, tiles * frames :, :] = jnp.concatenate([ends[0], ends[1]], axis=1)

    pl.when(me_ref[0] % 2 == 0)(lambda: pack(0, tiles * LANES, 0, 1))
    pl.when(me_ref[0] % 2 == 1)(lambda: pack(HALF, 0, 1, 0))


def normalized_blocks(series, subject_ids, me, slots, subjects):
    _, frames, width = series.shape
    depth = width * frames // LANES
    return pl.pallas_call(
        normalize_kernel,
        grid_spec=pltpu.PrefetchScalarGridSpec(
            num_scalar_prefetch=2,
            grid=(subjects,),
            in_specs=[pl.BlockSpec((1, frames, width), lambda s, ids, me: (ids[s], 0, 0))],
            out_specs=[
                pl.BlockSpec((1, 1, depth, LANES), lambda s, ids, me: (me[0], s, 0, 0)),
                pl.BlockSpec((1, width, frames), lambda s, ids, me: (s, 0, 0)),
            ],
        ),
        out_shape=[
            jax.ShapeDtypeStruct((slots, subjects, depth, LANES), jnp.bfloat16),
            jax.ShapeDtypeStruct((subjects, width, frames), jnp.bfloat16),
        ],
        name="normalize",
    )(subject_ids, me, series)


def gather_kernel(count, sizes, half, passed, in_ref, out_ref, send_sem, recv_sem):
    tall = count // 4
    me = lax.axis_index("blk")
    part = lax.axis_index("parts")
    z = me // 4
    x = (me // 2) % 2
    c = me % 2
    chunks = len(sizes)
    starts = [sum(sizes[:q]) for q in range(chunks)]
    held = sum(sizes)
    shares = [max(0, min(passed - start, size)) for start, size in zip(starts, sizes)]
    UP, DOWN, SIDE, TWIN, OVER, LATE = range(6)

    def device(zz, xx, cc):
        return (zz * 2 + xx) * 2 + cc

    target = {
        UP: {"blk": device(jnp.minimum(z + 1, tall - 1), x, c)},
        DOWN: {"blk": device(jnp.maximum(z - 1, 0), x, c)},
        SIDE: {"blk": device(z, 1 - x, c)},
        TWIN: {"blk": device(z, x, 1 - c)},
        OVER: {"parts": 1 - part},
        LATE: {"blk": device(z, x, 1 - c)},
    }
    has_up, has_down = z + 1 < tall, z > 0

    barrier = pltpu.get_barrier_semaphore()

    def greet(way):
        pl.semaphore_signal(
            barrier, inc=1, device_id=target[way], device_id_type=pl.DeviceIdType.MESH
        )

    greet(SIDE)
    greet(TWIN)
    greet(OVER)
    pl.when(has_up)(lambda: greet(UP))
    pl.when(has_down)(lambda: greet(DOWN))
    pl.semaphore_wait(barrier, 3 + has_up.astype(jnp.int32) + has_down.astype(jnp.int32))

    def copy(way, block, q):
        source = target_slots = pl.ds(starts[q], sizes[q])
        late = 0
        if way == OVER:
            source = pl.ds(starts[q], shares[q])
            target_slots = pl.ds(held + starts[q], shares[q])
            late = 1
        if way == LATE:
            source = target_slots = pl.ds(held + starts[q], shares[q])
            late = 1
        return pltpu.make_async_remote_copy(
            src_ref=out_ref.at[block, source],
            dst_ref=out_ref.at[block, target_slots],
            send_sem=send_sem.at[way, block, q],
            recv_sem=recv_sem.at[late, block, q],
            device_id=target[way],
            device_id_type=pl.DeviceIdType.MESH,
        )

    def send(way, block, q):
        copy(way, block, q).start()

    def arrived(block, q):
        copy(TWIN, block, q).wait_recv()

    def by_side(zz, at, q):
        if q < half:
            return jnp.bool_(True)
        low = jnp.logical_and(zz == 0, at > 0)
        high = jnp.logical_and(zz == tall - 1, at < tall - 1)
        return jnp.logical_not(jnp.logical_or(low, high))

    for q in range(chunks):
        pl.when(has_up)(lambda: send(UP, me, q))
        pl.when(has_down)(lambda: send(DOWN, me, q))
        pl.when(by_side(z, z, q))(lambda: send(SIDE, me, q))
        send(TWIN, me, q)
        if shares[q]:
            send(LATE, me, q)

    def visit(k, q, act):
        pl.when(z - k >= 0)(lambda: act(device(z - k, x, c), q, "low", k))
        pl.when(z + k < tall)(lambda: act(device(z + k, x, c), q, "high", k))
        if q >= half:
            pl.when(jnp.logical_and(z - k == -1, has_down))(
                lambda: act(device(0, 1 - x, c), q, "bottom", k)
            )
            pl.when(jnp.logical_and(z + k == tall, has_up))(
                lambda: act(device(tall - 1, 1 - x, c), q, "top", k)
            )
        pl.when(k == 1)(lambda: act(device(z, 1 - x, c), q, "side", k))
        low = z - k + 1
        pl.when(jnp.logical_and(jnp.logical_and(k > 1, low >= 0), by_side(low, z, q)))(
            lambda: act(device(low, 1 - x, c), q, "end", k)
        )
        high = z + k - 1
        pl.when(jnp.logical_and(jnp.logical_and(k > 1, high < tall), by_side(high, z, q)))(
            lambda: act(device(high, 1 - x, c), q, "end", k)
        )

    def relay(block, q, kind, k):
        arrived(block, q)
        if kind == "low":
            pl.when(has_up)(lambda: send(UP, block, q))
            pl.when(by_side(z - k, z, q))(lambda: send(SIDE, block, q))
        if kind == "high":
            pl.when(has_down)(lambda: send(DOWN, block, q))
            pl.when(by_side(z + k, z, q))(lambda: send(SIDE, block, q))
        if kind == "bottom":
            pl.when(has_up)(lambda: send(UP, block, q))
        if kind == "top":
            pl.when(has_down)(lambda: send(DOWN, block, q))
        if kind == "side" and q >= half:
            pl.when(jnp.logical_and(z == 0, has_up))(lambda: send(UP, block, q))
            pl.when(jnp.logical_and(z == tall - 1, has_down))(lambda: send(DOWN, block, q))
        send(TWIN, block, q)
        if shares[q]:
            send(OVER, block, q)

    def pass_on(block, q, kind, k):
        copy(OVER, block, q).wait_recv()
        send(LATE, block, q)

    def step(k, carry):
        for q in range(chunks):
            pl.when(k <= tall)(lambda: visit(k, q, relay))
            if shares[q]:
                pl.when(k >= 2)(lambda: visit(k - 1, q, pass_on))
        return carry

    lax.fori_loop(1, tall + (2 if passed else 1), step, 0)

    def finish(zz, carry):
        for q in range(chunks):
            own = device(zz, x, c)
            other = device(zz, 1 - x, c)
            arrived(device(zz, x, 1 - c), q)
            arrived(device(zz, 1 - x, 1 - c), q)
            copy(TWIN, own, q).wait_send()
            copy(TWIN, other, q).wait_send()
            pl.when(by_side(zz, z, q))(lambda: copy(SIDE, own, q).wait_send())
            pl.when(jnp.logical_and(has_up, zz <= z))(lambda: copy(UP, own, q).wait_send())
            pl.when(jnp.logical_and(has_down, zz >= z))(lambda: copy(DOWN, own, q).wait_send())
            if q >= half:
                pl.when(jnp.logical_and(has_up, zz == 0))(
                    lambda: copy(UP, other, q).wait_send()
                )
                pl.when(jnp.logical_and(has_down, zz == tall - 1))(
                    lambda: copy(DOWN, other, q).wait_send()
                )
            if shares[q]:
                copy(LATE, device(zz, x, 1 - c), q).wait_recv()
                copy(LATE, device(zz, 1 - x, 1 - c), q).wait_recv()
                copy(LATE, own, q).wait_send()
                copy(LATE, other, q).wait_send()
                pl.when(zz != z)(lambda: copy(OVER, own, q).wait_send())
                copy(OVER, other, q).wait_send()
        return carry

    lax.fori_loop(0, tall, finish, 0)


def chunk_sizes(slots):
    early = slots - slots // 2
    halves = [[early - early // 2, early // 2], [slots // 2 - slots // 4, slots // 4]]
    return [[size for size in half if size] for half in halves]


def gather(blocks, count, held, passed, collective_id):
    early, late = chunk_sizes(held)
    sizes = early + late
    return pl.pallas_call(
        functools.partial(gather_kernel, count, sizes, len(early), passed),
        out_shape=jax.ShapeDtypeStruct(blocks.shape, blocks.dtype),
        in_specs=[pl.BlockSpec(memory_space=pl.ANY)],
        out_specs=pl.BlockSpec(memory_space=pl.ANY),
        scratch_shapes=[
            pltpu.SemaphoreType.DMA((6, count, len(sizes))),
            pltpu.SemaphoreType.DMA((2, count, len(sizes))),
        ],
        input_output_aliases={0: 0},
        compiler_params=pltpu.CompilerParams(
            collective_id=collective_id, has_side_effects=True
        ),
        name=f"gather_{held}_{passed}",
    )(blocks)


def fisher_kernel(group, labels_ref, me_ref, slot_ref, left_ref, right_ref, out_ref, pair):
    step = pl.program_id(0)
    subjects, width, frames = left_ref.shape
    own = labels_ref[me_ref[0]]
    first = labels_ref[2 * step] == own
    second = labels_ref[2 * step + 1] == own
    either = jnp.logical_or(first, second)
    tiles, top = width // LANES, frames // 2
    low, high = tiles * LANES, (tiles + 1) * LANES
    bound = LIMIT * frames

    @pl.when(jnp.logical_not(either))
    def _():
        out_ref[...] = jnp.zeros_like(out_ref)

    @pl.when(either)
    def _():
        for s in range(subjects):
            for t in range(tiles):
                rows = slice(t * frames, (t + 1) * frames)
                pair[s, :, t * LANES : (t + 1) * LANES] = right_ref[0, s, rows, :]
                pair[s, :, high + t * LANES : high + (t + 1) * LANES] = right_ref[1, s, rows, :]
            a = right_ref[0, s, tiles * frames :, :].astype(jnp.float32)
            b = right_ref[1, s, tiles * frames :, :].astype(jnp.float32)
            front = lax.broadcasted_iota(jnp.int32, a.shape, 1) < HALF
            pair[s, :top, low:high] = jnp.where(front, a, b).astype(jnp.bfloat16)
            swapped = pltpu.roll(jnp.where(front, b, a), HALF, 1)
            pair[s, top:, low:high] = swapped.astype(jnp.bfloat16)

    def tile(start, size, wanted, mixed):
        @pl.when(jnp.logical_and(jnp.logical_not(wanted), either))
        def _():
            out_ref[:, start : start + size] = jnp.zeros((width, size), jnp.float32)

        @pl.when(wanted)
        def _():
            total = None
            for g in range(0, subjects, group):
                over = under = None
                for s in range(g, min(g + group, subjects)):
                    dot = jnp.dot(
                        left_ref[slot_ref[s]],
                        pair[slot_ref[s], :, start : start + size],
                        preferred_element_type=jnp.float32,
                    )
                    dot = jnp.clip(dot, -bound, bound)
                    plus, minus = frames + dot, frames - dot
                    over = plus if over is None else over * plus
                    under = minus if under is None else under * minus
                term = 0.5 * jnp.log(over / under)
                total = term if total is None else total + term
            if mixed:
                lane = start + lax.broadcasted_iota(jnp.int32, total.shape, 1)
                keep = jnp.where(lane < width, first.astype(jnp.int32), second.astype(jnp.int32))
                total = jnp.where(keep > 0, total, 0.0)
            out_ref[:, start : start + size] = total

    for start in range(0, low, 2 * LANES):
        size = min(2 * LANES, low - start)
        if size < 2 * LANES:
            tile(start, 2 * LANES, either, True)
        else:
            tile(start, size, first, False)
    if tiles % 2 == 0:
        tile(low, LANES, either, True)
    for start in range(high, 2 * width, 2 * LANES):
        tile(start, min(2 * LANES, 2 * width - start), second, False)


def correlate(left, blocks, labels, me, slot):
    count, subjects, depth, _ = blocks.shape
    _, width, frames = left.shape
    pairs = count // 2
    group = max(1, int(30 / math.log10(2 * frames)))

    def fetched(p, labels, me, slot):
        own = labels[me[0]]
        latest = jnp.int32(0)
        for t in range(pairs):
            hit = jnp.logical_or(labels[2 * t] == own, labels[2 * t + 1] == own)
            latest = jnp.where(jnp.logical_and(hit, t <= p), t, latest)
        return latest, 0, 0, 0

    return pl.pallas_call(
        functools.partial(fisher_kernel, group),
        grid_spec=pltpu.PrefetchScalarGridSpec(
            num_scalar_prefetch=3,
            grid=(pairs,),
            in_specs=[
                pl.BlockSpec((subjects, width, frames), lambda p, labels, me, slot: (0, 0, 0)),
                pl.BlockSpec((2, subjects, depth, LANES), fetched),
            ],
            out_specs=pl.BlockSpec((width, 2 * width), lambda p, labels, me, slot: (0, p)),
            scratch_shapes=[pltpu.VMEM((subjects, frames, 2 * width), jnp.bfloat16)],
        ),
        out_shape=jax.ShapeDtypeStruct((width, count * width), jnp.float32),
        compiler_params=pltpu.CompilerParams(vmem_limit_bytes=60 * 1024 * 1024),
        name="correlate",
    )(labels, me, slot, left, blocks)


def on_device(series, subject_ids, net_labels):
    count = lax.axis_size("blk")
    pool, frames, width = series.shape
    subjects = subject_ids.shape[0]
    packs = width % LANES == HALF and frames % 32 == 0
    fits = net_labels.shape[0] == count and count % 4 == 0 and lax.axis_size("parts") == 2
    if not (packs and fits and pool < 32 and subjects == FORMS[-1][0]):
        return plain(series, subject_ids, net_labels)
    me = lax.axis_index("blk").astype(jnp.int32)[None]
    part = lax.axis_index("parts").astype(jnp.int32)[None]
    others = lax.ppermute(subject_ids, "parts", [(0, 1), (1, 0)])
    listed, slot, form = distinct(pool, subject_ids, others, part)
    blocks, left = normalized_blocks(series, listed, me, count, subjects)
    runs = [
        functools.partial(gather, count=count, held=held, passed=passed, collective_id=i)
        for i, (held, passed) in enumerate(FORMS)
    ]
    blocks = lax.switch(form[0], runs, blocks)
    return correlate(left, blocks, net_labels, me, slot)


def solution(mesh):
    return jax.shard_map(
        on_device,
        mesh=mesh,
        in_specs=(P(None, None, "blk"), P("parts"), P()),
        out_specs=P(("parts", "blk"), None),
        check_vma=False,
    )
```

```python
import functools

import jax
import jax.numpy as jnp
from jax import lax
from jax.experimental import pallas as pl
from jax.experimental.pallas import tpu as pltpu
from jax.sharding import PartitionSpec as P

LIMIT = 0.999
LANES = 128
HALF = LANES // 2
FORMS = [(4, 2), (5, 2), (6, 2), (7, 1), (8, 0)]


def normalize(chosen):
    values = chosen.astype(jnp.float32)
    center = values - jnp.mean(values, axis=1, keepdims=True)
    spread = jnp.mean(center * center, axis=1, keepdims=True)
    return (center / jnp.sqrt(spread + 1e-05)).astype(jnp.bfloat16)


def fisher_sum(left, right):
    frames = left.shape[1]
    total = jnp.zeros((left.shape[2], right.shape[2]), jnp.float32)
    for subject in range(left.shape[0]):
        corr = (
            lax.dot_general(
                left[subject],
                right[subject],
                (((0,), (0,)), ((), ())),
                preferred_element_type=jnp.float32,
            )
            / frames
        )
        clipped = jnp.clip(corr, -LIMIT, LIMIT)
        total = total + 0.5 * jnp.log((1.0 + clipped) / (1.0 - clipped))
    return total


def plain(series, subject_ids, net_labels):
    normalized = normalize(jnp.take(series, subject_ids, axis=0))
    rows = normalized.shape[2]
    index = lax.axis_index("blk")
    count = lax.axis_size("blk")
    row_labels = jnp.repeat(net_labels, count * rows // net_labels.shape[0])
    own_labels = lax.dynamic_slice_in_dim(row_labels, index * rows, rows)
    gathered = lax.all_gather(normalized, "blk", axis=2, tiled=True)
    same = own_labels[:, None] == row_labels[None, :]
    return jnp.where(same, fisher_sum(normalized, gathered), 0.0)


def plan_kernel(
    pool, mine_ref, theirs_ref, first_ref, labels_ref, me_ref,
    list_ref, form_ref, order_ref, pairs_ref, number_ref, entry_ref, where_ref,
):
    subjects = mine_ref.shape[0]
    one, zero = jnp.int32(1), jnp.int32(0)

    def members(ref):
        bits = zero
        for s in range(subjects):
            bits = bits | (one << ref[s])
        return [(bits >> p) & 1 for p in range(pool)]

    mine, theirs = members(mine_ref), members(theirs_ref)
    own, other = sum(mine), sum(theirs)
    both = sum(a * b for a, b in zip(mine, theirs))
    form = jnp.int32(len(FORMS) - 1)
    held = jnp.int32(FORMS[-1][0])
    for index in reversed(range(len(FORMS) - 1)):
        carried, passed = FORMS[index]
        lack, give = jnp.maximum(own - carried, 0), jnp.maximum(other - carried, 0)
        fits = jnp.logical_and(jnp.maximum(lack, give) <= passed, lack + give <= both)
        form = jnp.where(fits, index, form)
        held = jnp.where(fits, carried, held)
    form_ref[0] = form
    lack, give = jnp.maximum(own - held, 0), jnp.maximum(other - held, 0)
    first = first_ref[0] == 0
    give_from = jnp.where(first, 0, lack)
    lack_from = jnp.where(first, give, 0)
    for s in range(list_ref.shape[0]):
        list_ref[s] = mine_ref[0]
    rank, plain_at = zero, give
    for p in range(pool):
        common = mine[p] * theirs[p]
        gives = jnp.logical_and(rank >= give_from, rank < give_from + give)
        gives = jnp.logical_and(gives, common == 1)
        lacks = jnp.logical_and(rank >= lack_from, rank < lack_from + lack)
        lacks = jnp.logical_and(lacks, common == 1)
        at = jnp.where(gives, rank - give_from, jnp.where(lacks, held + rank - lack_from, plain_at))
        kept = jnp.logical_and(mine[p] == 1, jnp.logical_not(jnp.logical_or(gives, lacks)))
        plain_at = plain_at + kept.astype(jnp.int32)
        rank = rank + common
        where_ref[p] = at
        list_ref[jnp.where(mine[p] == 1, at, subjects)] = jnp.int32(p)
    times = [sum((mine_ref[s] == p).astype(jnp.int32) for s in range(subjects)) for p in range(pool)]
    most = times[0]
    for t in times[1:]:
        most = jnp.maximum(most, t)
    squares = jnp.logical_and(most <= 2, own > subjects - 3)
    number_ref[0] = jnp.where(squares, own, subjects)
    for s in range(subjects):
        entry_ref[s] = where_ref[mine_ref[s]]

    @pl.when(squares)
    def _():
        many_at, one_at = zero, sum((t > 1).astype(jnp.int32) for t in times)
        for p in range(pool):
            many, single = times[p] > 1, times[p] == 1
            at = jnp.where(many, many_at, jnp.where(single, one_at, subjects))
            entry_ref[at] = where_ref[p]
            many_at = many_at + many.astype(jnp.int32)
            one_at = one_at + single.astype(jnp.int32)

    label = labels_ref[me_ref[0]]
    pairs = order_ref.shape[0] - 1
    found = zero
    for p in range(pairs):
        hit = jnp.logical_or(labels_ref[2 * p] == label, labels_ref[2 * p + 1] == label)
        order_ref[jnp.where(hit, found, pairs)] = jnp.int32(p)
        found = found + hit.astype(jnp.int32)
    pairs_ref[0] = found
    for p in range(pairs):
        order_ref[p] = order_ref[jnp.minimum(p, found - 1)]


def distinct(pool, mine, theirs, part, labels, me):
    subjects = mine.shape[0]
    sizes = [subjects + 1, 1, labels.shape[0] // 2 + 1, 1, 1, subjects + 1]
    return pl.pallas_call(
        functools.partial(plan_kernel, pool),
        out_shape=[jax.ShapeDtypeStruct((size,), jnp.int32) for size in sizes],
        in_specs=[pl.BlockSpec(memory_space=pltpu.SMEM)] * 5,
        out_specs=[pl.BlockSpec(memory_space=pltpu.SMEM)] * len(sizes),
        scratch_shapes=[pltpu.SMEM((pool,), jnp.int32)],
        name="plan",
    )(mine, theirs, part, labels, me)


def normalize_kernel(ids_ref, me_ref, series_ref, out_ref, turned_ref):
    values = series_ref[0].astype(jnp.float32)
    frames = values.shape[0]
    center = values - jnp.sum(values, axis=0, keepdims=True) / frames
    spread = jnp.sum(center * center, axis=0, keepdims=True) / frames
    result = center / jnp.sqrt(spread + 1e-05)
    packed = result.astype(jnp.bfloat16)
    turned_ref[0] = packed.T
    width = packed.shape[1]
    tiles, top = width // LANES, frames // 2

    def pack(first, edge, upper, lower):
        for t in range(tiles):
            start = first + t * LANES
            out_ref[0, 0, t * frames : (t + 1) * frames, :] = packed[:, start : start + LANES]
        ends = {upper: packed[:top, edge : edge + HALF], lower: packed[top:, edge : edge + HALF]}
        out_ref[0, 0, tiles * frames :, :] = jnp.concatenate([ends[0], ends[1]], axis=1)

    pl.when(me_ref[0] % 2 == 0)(lambda: pack(0, tiles * LANES, 0, 1))
    pl.when(me_ref[0] % 2 == 1)(lambda: pack(HALF, 0, 1, 0))


def normalized_blocks(series, subject_ids, me, slots, subjects):
    _, frames, width = series.shape
    depth = width * frames // LANES
    return pl.pallas_call(
        normalize_kernel,
        grid_spec=pltpu.PrefetchScalarGridSpec(
            num_scalar_prefetch=2,
            grid=(subjects,),
            in_specs=[pl.BlockSpec((1, frames, width), lambda s, ids, me: (ids[s], 0, 0))],
            out_specs=[
                pl.BlockSpec((1, 1, depth, LANES), lambda s, ids, me: (me[0], s, 0, 0)),
                pl.BlockSpec((1, width, frames), lambda s, ids, me: (s, 0, 0)),
            ],
        ),
        out_shape=[
            jax.ShapeDtypeStruct((slots, subjects, depth, LANES), jnp.bfloat16),
            jax.ShapeDtypeStruct((subjects, width, frames), jnp.bfloat16),
        ],
        name="normalize",
    )(subject_ids, me, series)


def gather_kernel(count, sizes, half, passed, in_ref, out_ref, send_sem, recv_sem):
    tall = count // 4
    me = lax.axis_index("blk")
    part = lax.axis_index("parts")
    z = me // 4
    x = (me // 2) % 2
    c = me % 2
    chunks = len(sizes)
    starts = [sum(sizes[:q]) for q in range(chunks)]
    held = sum(sizes)
    shares = [max(0, min(passed - start, size)) for start, size in zip(starts, sizes)]
    UP, DOWN, SIDE, TWIN, OVER, LATE = range(6)

    def device(zz, xx, cc):
        return (zz * 2 + xx) * 2 + cc

    target = {
        UP: {"blk": device(jnp.minimum(z + 1, tall - 1), x, c)},
        DOWN: {"blk": device(jnp.maximum(z - 1, 0), x, c)},
        SIDE: {"blk": device(z, 1 - x, c)},
        TWIN: {"blk": device(z, x, 1 - c)},
        OVER: {"parts": 1 - part},
        LATE: {"blk": device(z, x, 1 - c)},
    }
    has_up, has_down = z + 1 < tall, z > 0

    barrier = pltpu.get_barrier_semaphore()

    def greet(way):
        pl.semaphore_signal(
            barrier, inc=1, device_id=target[way], device_id_type=pl.DeviceIdType.MESH
        )

    greet(SIDE)
    greet(TWIN)
    greet(OVER)
    pl.when(has_up)(lambda: greet(UP))
    pl.when(has_down)(lambda: greet(DOWN))
    pl.semaphore_wait(barrier, 3 + has_up.astype(jnp.int32) + has_down.astype(jnp.int32))

    def copy(way, block, q):
        source = target_slots = pl.ds(starts[q], sizes[q])
        late = 0
        if way == OVER:
            source = pl.ds(starts[q], shares[q])
            target_slots = pl.ds(held + starts[q], shares[q])
            late = 1
        if way == LATE:
            source = target_slots = pl.ds(held + starts[q], shares[q])
            late = 1
        return pltpu.make_async_remote_copy(
            src_ref=out_ref.at[block, source],
            dst_ref=out_ref.at[block, target_slots],
            send_sem=send_sem.at[way, block, q],
            recv_sem=recv_sem.at[late, block, q],
            device_id=target[way],
            device_id_type=pl.DeviceIdType.MESH,
        )

    def send(way, block, q):
        copy(way, block, q).start()

    def arrived(block, q):
        copy(TWIN, block, q).wait_recv()

    def by_side(zz, at, q):
        if q < half:
            return jnp.bool_(True)
        low = jnp.logical_and(zz == 0, at > 0)
        high = jnp.logical_and(zz == tall - 1, at < tall - 1)
        return jnp.logical_not(jnp.logical_or(low, high))

    for q in range(chunks):
        pl.when(has_up)(lambda: send(UP, me, q))
        pl.when(has_down)(lambda: send(DOWN, me, q))
        pl.when(by_side(z, z, q))(lambda: send(SIDE, me, q))
        send(TWIN, me, q)
        if shares[q]:
            send(LATE, me, q)

    def visit(k, q, act):
        pl.when(z - k >= 0)(lambda: act(device(z - k, x, c), q, "low", k))
        pl.when(z + k < tall)(lambda: act(device(z + k, x, c), q, "high", k))
        if q >= half:
            pl.when(jnp.logical_and(z - k == -1, has_down))(
                lambda: act(device(0, 1 - x, c), q, "bottom", k)
            )
            pl.when(jnp.logical_and(z + k == tall, has_up))(
                lambda: act(device(tall - 1, 1 - x, c), q, "top", k)
            )
        pl.when(k == 1)(lambda: act(device(z, 1 - x, c), q, "side", k))
        low = z - k + 1
        pl.when(jnp.logical_and(jnp.logical_and(k > 1, low >= 0), by_side(low, z, q)))(
            lambda: act(device(low, 1 - x, c), q, "end", k)
        )
        high = z + k - 1
        pl.when(jnp.logical_and(jnp.logical_and(k > 1, high < tall), by_side(high, z, q)))(
            lambda: act(device(high, 1 - x, c), q, "end", k)
        )

    def relay(block, q, kind, k):
        arrived(block, q)
        if kind == "low":
            pl.when(has_up)(lambda: send(UP, block, q))
            pl.when(by_side(z - k, z, q))(lambda: send(SIDE, block, q))
        if kind == "high":
            pl.when(has_down)(lambda: send(DOWN, block, q))
            pl.when(by_side(z + k, z, q))(lambda: send(SIDE, block, q))
        if kind == "bottom":
            pl.when(has_up)(lambda: send(UP, block, q))
        if kind == "top":
            pl.when(has_down)(lambda: send(DOWN, block, q))
        if kind == "side" and q >= half:
            pl.when(jnp.logical_and(z == 0, has_up))(lambda: send(UP, block, q))
            pl.when(jnp.logical_and(z == tall - 1, has_down))(lambda: send(DOWN, block, q))
        send(TWIN, block, q)
        if shares[q]:
            send(OVER, block, q)

    def pass_on(block, q, kind, k):
        copy(OVER, block, q).wait_recv()
        send(LATE, block, q)

    def step(k, carry):
        for q in range(chunks):
            pl.when(k <= tall)(lambda: visit(k, q, relay))
            if shares[q]:
                pl.when(k >= 2)(lambda: visit(k - 1, q, pass_on))
        return carry

    lax.fori_loop(1, tall + (2 if passed else 1), step, 0)

    def finish(zz, carry):
        for q in range(chunks):
            own = device(zz, x, c)
            other = device(zz, 1 - x, c)
            arrived(device(zz, x, 1 - c), q)
            arrived(device(zz, 1 - x, 1 - c), q)
            copy(TWIN, own, q).wait_send()
            copy(TWIN, other, q).wait_send()
            pl.when(by_side(zz, z, q))(lambda: copy(SIDE, own, q).wait_send())
            pl.when(jnp.logical_and(has_up, zz <= z))(lambda: copy(UP, own, q).wait_send())
            pl.when(jnp.logical_and(has_down, zz >= z))(lambda: copy(DOWN, own, q).wait_send())
            if q >= half:
                pl.when(jnp.logical_and(has_up, zz == 0))(
                    lambda: copy(UP, other, q).wait_send()
                )
                pl.when(jnp.logical_and(has_down, zz == tall - 1))(
                    lambda: copy(DOWN, other, q).wait_send()
                )
            if shares[q]:
                copy(LATE, device(zz, x, 1 - c), q).wait_recv()
                copy(LATE, device(zz, 1 - x, 1 - c), q).wait_recv()
                copy(LATE, own, q).wait_send()
                copy(LATE, other, q).wait_send()
                pl.when(zz != z)(lambda: copy(OVER, own, q).wait_send())
                copy(OVER, other, q).wait_send()
        return carry

    lax.fori_loop(0, tall, finish, 0)


def chunk_sizes(slots, passed):
    early = slots - slots // 2
    rest = early - passed
    halves = [[1] * passed + [rest - rest // 2, rest // 2], [slots // 2 - slots // 4, slots // 4]]
    return [[size for size in half if size] for half in halves]


def gather(blocks, count, held, passed, collective_id):
    early, late = chunk_sizes(held, passed)
    sizes = early + late
    return pl.pallas_call(
        functools.partial(gather_kernel, count, sizes, len(early), passed),
        out_shape=jax.ShapeDtypeStruct(blocks.shape, blocks.dtype),
        in_specs=[pl.BlockSpec(memory_space=pl.ANY)],
        out_specs=pl.BlockSpec(memory_space=pl.ANY),
        scratch_shapes=[
            pltpu.SemaphoreType.DMA((6, count, len(sizes))),
            pltpu.SemaphoreType.DMA((2, count, len(sizes))),
        ],
        input_output_aliases={0: 0},
        compiler_params=pltpu.CompilerParams(
            collective_id=collective_id, has_side_effects=True
        ),
        name=f"gather_{held}_{passed}",
    )(blocks)


def fisher_kernel(
    counts, labels_ref, me_ref, order_ref, pairs_ref, number_ref, entry_ref,
    left_ref, right_ref, out_ref, middle, zeros, done, zero_sem, done_sem,
):
    step = pl.program_id(0)
    subjects, width, frames = left_ref.shape
    pairs = order_ref.shape[0] - 1
    own = labels_ref[me_ref[0]]
    active = step < pairs_ref[0]
    spot = order_ref[step]
    first = jnp.logical_and(active, labels_ref[2 * spot] == own)
    second = jnp.logical_and(active, labels_ref[2 * spot + 1] == own)
    tiles, top = width // LANES, frames // 2
    low, high = tiles * LANES, (tiles + 1) * LANES
    bound = LIMIT * frames
    now = step % 2

    def columns(p):
        return out_ref.at[:, pl.ds(pl.multiple_of(p * 2 * width, LANES), 2 * width)]

    def blank(p):
        return pltpu.make_async_copy(zeros, columns(p), zero_sem.at[p])

    def result(slot, p):
        return pltpu.make_async_copy(done.at[slot], columns(p), done_sem.at[slot])

    def empty(p):
        return jnp.logical_not(
            jnp.logical_or(labels_ref[2 * p] == own, labels_ref[2 * p + 1] == own)
        )

    @pl.when(step == 0)
    def _():
        zeros[...] = jnp.zeros_like(zeros)
        for p in range(pairs):
            pl.when(empty(p))(lambda: blank(p).start())

    @pl.when(jnp.logical_and(active, step >= 2))
    def _():
        result(now, order_ref[jnp.maximum(step - 2, 0)]).wait()

    @pl.when(active)
    def _():
        for s in range(subjects):
            a = right_ref[0, s, tiles * frames :, :].astype(jnp.float32)
            b = right_ref[1, s, tiles * frames :, :].astype(jnp.float32)
            front = lax.broadcasted_iota(jnp.int32, a.shape, 1) < HALF
            middle[s, :top, :] = jnp.where(front, a, b).astype(jnp.bfloat16)
            swapped = pltpu.roll(jnp.where(front, b, a), HALF, 1)
            middle[s, top:, :] = swapped.astype(jnp.bfloat16)

    def part(slot, t):
        if t == tiles:
            return middle[slot]
        block, row = (0, t) if t < tiles else (1, t - tiles - 1)
        return right_ref[block, slot, row * frames : (row + 1) * frames, :]

    def tile(span, wanted, mixed):
        start, size = span[0] * LANES, len(span) * LANES

        def value(count):
            over = under = None
            for s in range(count):
                slot = entry_ref[s]
                right = jnp.concatenate([part(slot, t) for t in span], axis=1)
                dot = jnp.dot(left_ref[slot], right, preferred_element_type=jnp.float32)
                dot = jnp.clip(dot, -bound, bound)
                plus, minus = frames + dot, frames - dot
                if s < subjects - count:
                    plus, minus = plus * plus, minus * minus
                over = plus if over is None else over * plus
                under = minus if under is None else under * minus
            return 0.5 * jnp.log(over / under)

        @pl.when(jnp.logical_and(active, jnp.logical_not(wanted)))
        def _():
            done[now, :, start : start + size] = jnp.zeros((width, size), jnp.float32)

        for count in counts:
            @pl.when(jnp.logical_and(wanted, number_ref[0] == count))
            def _():
                total = value(count)
                if mixed:
                    lane = start + lax.broadcasted_iota(jnp.int32, total.shape, 1)
                    keep = jnp.where(
                        lane < width, first.astype(jnp.int32), second.astype(jnp.int32)
                    )
                    total = jnp.where(keep > 0, total, 0.0)
                done[now, :, start : start + size] = total

    either = jnp.logical_or(first, second)
    for t in range(0, 2 * tiles + 1, 2):
        span = [u for u in (t, t + 1) if u <= 2 * tiles]
        if tiles in span:
            tile(span, either, True)
        else:
            tile(span, first if span[-1] < tiles else second, False)

    pl.when(active)(lambda: result(now, spot).start())

    @pl.when(step == pairs - 1)
    def _():
        last = pairs_ref[0] - 1
        result(last % 2, order_ref[last]).wait()

        @pl.when(last >= 1)
        def _():
            result((last - 1) % 2, order_ref[jnp.maximum(last - 1, 0)]).wait()

        for p in range(pairs):
            pl.when(empty(p))(lambda: blank(p).wait())


def correlate(left, blocks, labels, me, table):
    order, matched, number, entry = table
    count, subjects, depth, _ = blocks.shape
    _, width, frames = left.shape
    pairs = count // 2
    return pl.pallas_call(
        functools.partial(fisher_kernel, [subjects - again for again in range(3)]),
        grid_spec=pltpu.PrefetchScalarGridSpec(
            num_scalar_prefetch=6,
            grid=(pairs,),
            in_specs=[
                pl.BlockSpec((subjects, width, frames), lambda p, *refs: (0, 0, 0)),
                pl.BlockSpec((2, subjects, depth, LANES), lambda p, lb, me, order, *refs: (order[p], 0, 0, 0)),
            ],
            out_specs=pl.BlockSpec(memory_space=pl.ANY),
            scratch_shapes=[
                pltpu.VMEM((subjects, frames, LANES), jnp.bfloat16),
                pltpu.VMEM((width, 2 * width), jnp.float32),
                pltpu.VMEM((2, width, 2 * width), jnp.float32),
                pltpu.SemaphoreType.DMA((pairs,)),
                pltpu.SemaphoreType.DMA((2,)),
            ],
        ),
        out_shape=jax.ShapeDtypeStruct((width, count * width), jnp.float32),
        compiler_params=pltpu.CompilerParams(vmem_limit_bytes=60 * 1024 * 1024),
        name="correlate",
    )(labels, me, order, matched, number, entry, left, blocks)


def on_device(series, subject_ids, net_labels):
    count = lax.axis_size("blk")
    pool, frames, width = series.shape
    subjects = subject_ids.shape[0]
    packs = width % LANES == HALF and frames % 32 == 0
    fits = net_labels.shape[0] == count and count % 4 == 0 and lax.axis_size("parts") == 2
    if not (packs and fits and pool < 32 and subjects == FORMS[-1][0]):
        return plain(series, subject_ids, net_labels)
    me = lax.axis_index("blk").astype(jnp.int32)[None]
    part = lax.axis_index("parts").astype(jnp.int32)[None]
    others = lax.ppermute(subject_ids, "parts", [(0, 1), (1, 0)])
    listed, form, *table = distinct(pool, subject_ids, others, part, net_labels, me)
    blocks, left = normalized_blocks(series, listed, me, count, subjects)
    runs = [
        functools.partial(gather, count=count, held=held, passed=passed, collective_id=i)
        for i, (held, passed) in enumerate(FORMS)
    ]
    blocks = lax.switch(form[0], runs, blocks)
    return correlate(left, blocks, net_labels, me, table)


def solution(mesh):
    return jax.shard_map(
        on_device,
        mesh=mesh,
        in_specs=(P(None, None, "blk"), P("parts"), P()),
        out_specs=P(("parts", "blk"), None),
        check_vma=False,
    )
```

```python
import functools

import jax
import jax.numpy as jnp
from jax import lax
from jax.experimental import pallas as pl
from jax.experimental.pallas import tpu as pltpu
from jax.sharding import PartitionSpec as P

LIMIT = 0.999
LANES = 128
HALF = LANES // 2
FORMS = [(4, 2), (5, 2), (6, 2), (8, 0)]


def normalize(chosen):
    values = chosen.astype(jnp.float32)
    center = values - jnp.mean(values, axis=1, keepdims=True)
    spread = jnp.mean(center * center, axis=1, keepdims=True)
    return (center / jnp.sqrt(spread + 1e-05)).astype(jnp.bfloat16)


def fisher_sum(left, right):
    frames = left.shape[1]
    total = jnp.zeros((left.shape[2], right.shape[2]), jnp.float32)
    for subject in range(left.shape[0]):
        corr = (
            lax.dot_general(
                left[subject],
                right[subject],
                (((0,), (0,)), ((), ())),
                preferred_element_type=jnp.float32,
            )
            / frames
        )
        clipped = jnp.clip(corr, -LIMIT, LIMIT)
        total = total + 0.5 * jnp.log((1.0 + clipped) / (1.0 - clipped))
    return total


def plain(series, subject_ids, net_labels):
    normalized = normalize(jnp.take(series, subject_ids, axis=0))
    rows = normalized.shape[2]
    index = lax.axis_index("blk")
    count = lax.axis_size("blk")
    row_labels = jnp.repeat(net_labels, count * rows // net_labels.shape[0])
    own_labels = lax.dynamic_slice_in_dim(row_labels, index * rows, rows)
    gathered = lax.all_gather(normalized, "blk", axis=2, tiled=True)
    same = own_labels[:, None] == row_labels[None, :]
    return jnp.where(same, fisher_sum(normalized, gathered), 0.0)


def plan_kernel(
    pool, mine_ref, theirs_ref, first_ref, labels_ref, me_ref,
    list_ref, form_ref, order_ref, pairs_ref, number_ref, entry_ref,
    where_ref,
):
    subjects = mine_ref.shape[0]
    one, zero = jnp.int32(1), jnp.int32(0)

    def members(ref):
        bits = zero
        for s in range(subjects):
            bits = bits | (one << ref[s])
        return [(bits >> p) & 1 for p in range(pool)]

    mine, theirs = members(mine_ref), members(theirs_ref)
    own, other = sum(mine), sum(theirs)
    both = sum(a * b for a, b in zip(mine, theirs))
    form = jnp.int32(len(FORMS) - 1)
    held = jnp.int32(FORMS[-1][0])
    for index in reversed(range(len(FORMS) - 1)):
        carried, passed = FORMS[index]
        lack, give = jnp.maximum(own - carried, 0), jnp.maximum(other - carried, 0)
        fits = jnp.logical_and(jnp.maximum(lack, give) <= passed, lack + give <= both)
        form = jnp.where(fits, index, form)
        held = jnp.where(fits, carried, held)
    form_ref[0] = form
    lack, give = jnp.maximum(own - held, 0), jnp.maximum(other - held, 0)
    first = first_ref[0] == 0
    give_from = jnp.where(first, 0, lack)
    lack_from = jnp.where(first, give, 0)
    for s in range(list_ref.shape[0]):
        list_ref[s] = mine_ref[0]
    rank, plain_at = zero, give
    for p in range(pool):
        common = mine[p] * theirs[p]
        gives = jnp.logical_and(rank >= give_from, rank < give_from + give)
        gives = jnp.logical_and(gives, common == 1)
        lacks = jnp.logical_and(rank >= lack_from, rank < lack_from + lack)
        lacks = jnp.logical_and(lacks, common == 1)
        at = jnp.where(gives, rank - give_from, jnp.where(lacks, held + rank - lack_from, plain_at))
        kept = jnp.logical_and(mine[p] == 1, jnp.logical_not(jnp.logical_or(gives, lacks)))
        plain_at = plain_at + kept.astype(jnp.int32)
        rank = rank + common
        where_ref[p] = at
        list_ref[jnp.where(mine[p] == 1, at, subjects)] = jnp.int32(p)
    times = [sum((mine_ref[s] == p).astype(jnp.int32) for s in range(subjects)) for p in range(pool)]
    most = times[0]
    for t in times[1:]:
        most = jnp.maximum(most, t)
    squares = jnp.logical_and(most <= 2, own > subjects - 3)
    number_ref[0] = jnp.where(squares, own, subjects)
    for s in range(subjects):
        entry_ref[s] = where_ref[mine_ref[s]]

    @pl.when(squares)
    def _():
        many_at, one_at = zero, sum((t > 1).astype(jnp.int32) for t in times)
        for p in range(pool):
            many, single = times[p] > 1, times[p] == 1
            at = jnp.where(many, many_at, jnp.where(single, one_at, subjects))
            entry_ref[at] = where_ref[p]
            many_at = many_at + many.astype(jnp.int32)
            one_at = one_at + single.astype(jnp.int32)

    label = labels_ref[me_ref[0]]
    pairs = order_ref.shape[0] - 1
    found = zero
    for p in range(pairs):
        front, back = labels_ref[2 * p] == label, labels_ref[2 * p + 1] == label
        hit = jnp.logical_or(front, back)
        at = jnp.where(hit, found, pairs)
        order_ref[at] = jnp.int32(p)
        found = found + hit.astype(jnp.int32)
    pairs_ref[0] = found


def distinct(pool, mine, theirs, part, labels, me):
    subjects = mine.shape[0]
    spots = labels.shape[0] // 2 + 1
    sizes = [subjects + 1, 1, spots, 1, 1, subjects + 1]
    return pl.pallas_call(
        functools.partial(plan_kernel, pool),
        out_shape=[jax.ShapeDtypeStruct((size,), jnp.int32) for size in sizes],
        in_specs=[pl.BlockSpec(memory_space=pltpu.SMEM)] * 5,
        out_specs=[pl.BlockSpec(memory_space=pltpu.SMEM)] * len(sizes),
        scratch_shapes=[pltpu.SMEM((pool,), jnp.int32)],
        name="plan",
    )(mine, theirs, part, labels, me)


def gather_kernel(
    count, sizes, half, passed, ids_ref, series_ref, out_ref, left_ref,
    pool, packed, turned, load_sem, store_sem, send_sem, recv_sem,
):
    tall = count // 4
    me = lax.axis_index("blk")
    part = lax.axis_index("parts")
    z = me // 4
    x = (me // 2) % 2
    c = me % 2
    chunks = len(sizes)
    starts = [sum(sizes[:q]) for q in range(chunks)]
    held = sum(sizes)
    shares = [max(0, min(passed - start, size)) for start, size in zip(starts, sizes)]
    UP, DOWN, SIDE, TWIN, OVER, LATE = range(6)

    def device(zz, xx, cc):
        return (zz * 2 + xx) * 2 + cc

    target = {
        UP: {"blk": device(jnp.minimum(z + 1, tall - 1), x, c)},
        DOWN: {"blk": device(jnp.maximum(z - 1, 0), x, c)},
        SIDE: {"blk": device(z, 1 - x, c)},
        TWIN: {"blk": device(z, x, 1 - c)},
        OVER: {"parts": 1 - part},
        LATE: {"blk": device(z, x, 1 - c)},
    }
    has_up, has_down = z + 1 < tall, z > 0

    load = pltpu.make_async_copy(series_ref, pool, load_sem)
    load.start()
    barrier = pltpu.get_barrier_semaphore()

    def greet(way):
        pl.semaphore_signal(
            barrier, inc=1, device_id=target[way], device_id_type=pl.DeviceIdType.MESH
        )

    greet(SIDE)
    greet(TWIN)
    greet(OVER)
    pl.when(has_up)(lambda: greet(UP))
    pl.when(has_down)(lambda: greet(DOWN))
    pl.semaphore_wait(barrier, 3 + has_up.astype(jnp.int32) + has_down.astype(jnp.int32))

    def copy(way, block, q):
        source = target_slots = pl.ds(starts[q], sizes[q])
        late = 0
        if way == OVER:
            source = pl.ds(starts[q], shares[q])
            target_slots = pl.ds(held + starts[q], shares[q])
            late = 1
        if way == LATE:
            source = target_slots = pl.ds(held + starts[q], shares[q])
            late = 1
        return pltpu.make_async_remote_copy(
            src_ref=out_ref.at[block, source],
            dst_ref=out_ref.at[block, target_slots],
            send_sem=send_sem.at[way, block, q],
            recv_sem=recv_sem.at[late, block, q],
            device_id=target[way],
            device_id_type=pl.DeviceIdType.MESH,
        )

    def send(way, block, q):
        copy(way, block, q).start()

    def arrived(block, q):
        copy(TWIN, block, q).wait_recv()

    def by_side(zz, at, q):
        if q < half:
            return jnp.bool_(True)
        low = jnp.logical_and(zz == 0, at > 0)
        high = jnp.logical_and(zz == tall - 1, at < tall - 1)
        return jnp.logical_not(jnp.logical_or(low, high))

    def stores(s):
        slot = s % 2
        return [
            pltpu.make_async_copy(packed.at[slot], out_ref.at[me, s], store_sem.at[0, slot]),
            pltpu.make_async_copy(turned.at[slot], left_ref.at[s], store_sem.at[1, slot]),
        ]

    def normalize(s):
        slot = s % 2
        values = pool[ids_ref[s]].astype(jnp.float32)
        frames, width = values.shape
        center = values - jnp.sum(values, axis=0, keepdims=True) / frames
        spread = jnp.sum(center * center, axis=0, keepdims=True) / frames
        result = (center * (1.0 / jnp.sqrt(spread + 1e-05))).astype(jnp.bfloat16)
        turned[slot] = result.T
        tiles, top = width // LANES, frames // 2

        def pack(first, edge, upper, lower):
            for t in range(tiles):
                start = first + t * LANES
                packed[slot, t * frames : (t + 1) * frames, :] = result[:, start : start + LANES]
            ends = {upper: result[:top, edge : edge + HALF], lower: result[top:, edge : edge + HALF]}
            packed[slot, tiles * frames :, :] = jnp.concatenate([ends[0], ends[1]], axis=1)

        pl.when(c == 0)(lambda: pack(0, tiles * LANES, 0, 1))
        pl.when(c == 1)(lambda: pack(HALF, 0, 1, 0))

    def prepare(s, carry):
        @pl.when(s < held + passed)
        def _():
            normalize(s)
            for copy_out in stores(s):
                copy_out.start()

        @pl.when(s >= 1)
        def _():
            for copy_out in stores(s - 1):
                copy_out.wait()
            for q in range(chunks):
                @pl.when(s == starts[q] + sizes[q])
                def _():
                    pl.when(has_up)(lambda: send(UP, me, q))
                    pl.when(has_down)(lambda: send(DOWN, me, q))
                    pl.when(by_side(z, z, q))(lambda: send(SIDE, me, q))
                    send(TWIN, me, q)

                if shares[q]:
                    pl.when(s == held + starts[q] + shares[q])(lambda: send(LATE, me, q))

        return carry

    load.wait()
    lax.fori_loop(0, held + passed + 1, prepare, 0)

    def visit(k, q, act):
        pl.when(z - k >= 0)(lambda: act(device(z - k, x, c), q, "low", k))
        pl.when(z + k < tall)(lambda: act(device(z + k, x, c), q, "high", k))
        if q >= half:
            pl.when(jnp.logical_and(z - k == -1, has_down))(
                lambda: act(device(0, 1 - x, c), q, "bottom", k)
            )
            pl.when(jnp.logical_and(z + k == tall, has_up))(
                lambda: act(device(tall - 1, 1 - x, c), q, "top", k)
            )
        pl.when(k == 1)(lambda: act(device(z, 1 - x, c), q, "side", k))
        low = z - k + 1
        pl.when(jnp.logical_and(jnp.logical_and(k > 1, low >= 0), by_side(low, z, q)))(
            lambda: act(device(low, 1 - x, c), q, "end", k)
        )
        high = z + k - 1
        pl.when(jnp.logical_and(jnp.logical_and(k > 1, high < tall), by_side(high, z, q)))(
            lambda: act(device(high, 1 - x, c), q, "end", k)
        )

    def relay(block, q, kind, k):
        arrived(block, q)
        if kind == "low":
            pl.when(has_up)(lambda: send(UP, block, q))
            pl.when(by_side(z - k, z, q))(lambda: send(SIDE, block, q))
        if kind == "high":
            pl.when(has_down)(lambda: send(DOWN, block, q))
            pl.when(by_side(z + k, z, q))(lambda: send(SIDE, block, q))
        if kind == "bottom":
            pl.when(has_up)(lambda: send(UP, block, q))
        if kind == "top":
            pl.when(has_down)(lambda: send(DOWN, block, q))
        if kind == "side" and q >= half:
            pl.when(jnp.logical_and(z == 0, has_up))(lambda: send(UP, block, q))
            pl.when(jnp.logical_and(z == tall - 1, has_down))(lambda: send(DOWN, block, q))
        send(TWIN, block, q)
        if shares[q]:
            send(OVER, block, q)

    def pass_on(block, q, kind, k):
        copy(OVER, block, q).wait_recv()
        send(LATE, block, q)

    def step(k, carry):
        for q in range(chunks):
            pl.when(k <= tall)(lambda: visit(k, q, relay))
            if shares[q]:
                pl.when(k >= 2)(lambda: visit(k - 1, q, pass_on))
        return carry

    lax.fori_loop(1, tall + (2 if passed else 1), step, 0)

    def finish(zz, carry):
        for q in range(chunks):
            own = device(zz, x, c)
            other = device(zz, 1 - x, c)
            arrived(device(zz, x, 1 - c), q)
            arrived(device(zz, 1 - x, 1 - c), q)
            copy(TWIN, own, q).wait_send()
            copy(TWIN, other, q).wait_send()
            pl.when(by_side(zz, z, q))(lambda: copy(SIDE, own, q).wait_send())
            pl.when(jnp.logical_and(has_up, zz <= z))(lambda: copy(UP, own, q).wait_send())
            pl.when(jnp.logical_and(has_down, zz >= z))(lambda: copy(DOWN, own, q).wait_send())
            if q >= half:
                pl.when(jnp.logical_and(has_up, zz == 0))(
                    lambda: copy(UP, other, q).wait_send()
                )
                pl.when(jnp.logical_and(has_down, zz == tall - 1))(
                    lambda: copy(DOWN, other, q).wait_send()
                )
            if shares[q]:
                copy(LATE, device(zz, x, 1 - c), q).wait_recv()
                copy(LATE, device(zz, 1 - x, 1 - c), q).wait_recv()
                copy(LATE, own, q).wait_send()
                copy(LATE, other, q).wait_send()
                pl.when(zz != z)(lambda: copy(OVER, own, q).wait_send())
                copy(OVER, other, q).wait_send()
        return carry

    lax.fori_loop(0, tall, finish, 0)


def chunk_sizes(slots, passed):
    early = slots - slots // 2
    rest = early - passed
    halves = [[1] * passed + [rest - rest // 2, rest // 2], [slots // 2 - slots // 4, slots // 4]]
    return [[size for size in half if size] for half in halves]


def gather(listed, series, count, subjects, held, passed, collective_id):
    early, late = chunk_sizes(held, passed)
    sizes = early + late
    pool, frames, width = series.shape
    depth = width * frames // LANES
    return pl.pallas_call(
        functools.partial(gather_kernel, count, sizes, len(early), passed),
        out_shape=[
            jax.ShapeDtypeStruct((count, subjects, depth, LANES), jnp.bfloat16),
            jax.ShapeDtypeStruct((subjects, width, frames), jnp.bfloat16),
        ],
        in_specs=[pl.BlockSpec(memory_space=pltpu.SMEM), pl.BlockSpec(memory_space=pl.ANY)],
        out_specs=[pl.BlockSpec(memory_space=pl.ANY)] * 2,
        scratch_shapes=[
            pltpu.VMEM((pool, frames, width), jnp.bfloat16),
            pltpu.VMEM((2, depth, LANES), jnp.bfloat16),
            pltpu.VMEM((2, width, frames), jnp.bfloat16),
            pltpu.SemaphoreType.DMA,
            pltpu.SemaphoreType.DMA((2, 2)),
            pltpu.SemaphoreType.DMA((6, count, len(sizes))),
            pltpu.SemaphoreType.DMA((2, count, len(sizes))),
        ],
        compiler_params=pltpu.CompilerParams(
            collective_id=collective_id, has_side_effects=True
        ),
        name=f"gather_{held}_{passed}",
    )(listed, series)


def fisher_kernel(
    counts, labels_ref, me_ref, order_ref, matched_ref, number_ref, entry_ref,
    source_ref, blocks_ref, out_ref, left_ref, right, middle, zeros, done,
    zero_sem, done_sem, right_sem, left_sem,
):
    subjects, width, frames = left_ref.shape
    pairs = order_ref.shape[0] - 1
    own = labels_ref[me_ref[0]]
    tiles, top = width // LANES, frames // 2
    bound = LIMIT * frames
    strip = zeros.shape[0]
    matched = matched_ref[0]

    def columns(p):
        return pl.ds(pl.multiple_of(p * 2 * width, LANES), 2 * width)

    def blank(p, r):
        target = out_ref.at[r * strip : (r + 1) * strip, columns(p)]
        return pltpu.make_async_copy(zeros, target, zero_sem.at[p, r])

    def result(slot, p):
        return pltpu.make_async_copy(done.at[slot], out_ref.at[:, columns(p)], done_sem.at[slot])

    def empty(p):
        return jnp.logical_not(
            jnp.logical_or(labels_ref[2 * p] == own, labels_ref[2 * p + 1] == own)
        )

    def fetch(step, act):
        slot = step % 2
        for side in range(2):
            block = 2 * order_ref[step] + side

            @pl.when(labels_ref[block] == own)
            def _():
                act(
                    pltpu.make_async_copy(
                        blocks_ref.at[block], right.at[slot, side], right_sem.at[slot, side]
                    )
                )

    whole = pltpu.make_async_copy(source_ref, left_ref, left_sem)
    whole.start()
    fetch(0, lambda copy: copy.start())
    zeros[...] = jnp.zeros_like(zeros)

    def blanks(act):
        for p in range(pairs):
            @pl.when(empty(p))
            def _():
                for r in range(width // strip):
                    act(blank(p, r))

    def body(step, carry):
        spot = order_ref[step]
        first = labels_ref[2 * spot] == own
        second = labels_ref[2 * spot + 1] == own
        now = step % 2
        fetch(step, lambda copy: copy.wait())
        pl.when(step + 1 < matched)(lambda: fetch(step + 1, lambda copy: copy.start()))
        @pl.when(step == 0)
        def _():
            whole.wait()
            blanks(lambda copy: copy.start())

        pl.when(step >= 2)(lambda: result(now, spot).wait())

        for s in range(subjects):
            a = right[now, 0, s, tiles * frames :, :].astype(jnp.float32)
            b = right[now, 1, s, tiles * frames :, :].astype(jnp.float32)
            front = lax.broadcasted_iota(jnp.int32, a.shape, 1) < HALF
            middle[s, :top, :] = jnp.where(front, a, b).astype(jnp.bfloat16)
            swapped = pltpu.roll(jnp.where(front, b, a), HALF, 1)
            middle[s, top:, :] = swapped.astype(jnp.bfloat16)

        def part(slot, t):
            if t == tiles:
                return middle[slot]
            side, row = (0, t) if t < tiles else (1, t - tiles - 1)
            return right[now, side, slot, row * frames : (row + 1) * frames, :]

        def tile(span, wanted, mixed):
            start, size = span[0] * LANES, len(span) * LANES

            def value(count):
                over = under = None
                for s in range(count):
                    slot = entry_ref[s]
                    these = jnp.concatenate([part(slot, t) for t in span], axis=1)
                    dot = jnp.dot(left_ref[slot], these, preferred_element_type=jnp.float32)
                    dot = jnp.clip(dot, -bound, bound)
                    plus, minus = frames + dot, frames - dot
                    if s < subjects - count:
                        plus, minus = plus * plus, minus * minus
                    over = plus if over is None else over * plus
                    under = minus if under is None else under * minus
                return 0.5 * jnp.log(over / under)

            @pl.when(jnp.logical_not(wanted))
            def _():
                done[now, :, start : start + size] = jnp.zeros((width, size), jnp.float32)

            for count in counts:
                @pl.when(jnp.logical_and(wanted, number_ref[0] == count))
                def _():
                    total = value(count)
                    if mixed:
                        lane = start + lax.broadcasted_iota(jnp.int32, total.shape, 1)
                        keep = jnp.where(
                            lane < width, first.astype(jnp.int32), second.astype(jnp.int32)
                        )
                        total = jnp.where(keep > 0, total, 0.0)
                    done[now, :, start : start + size] = total

        for t in range(0, 2 * tiles + 1, 2):
            span = [u for u in (t, t + 1) if u <= 2 * tiles]
            if tiles in span:
                tile(span, jnp.logical_or(first, second), True)
            else:
                tile(span, first if span[-1] < tiles else second, False)

        result(now, spot).start()
        return carry

    lax.fori_loop(0, matched, body, 0)
    final = matched - 1
    result(final % 2, order_ref[final]).wait()

    @pl.when(final >= 1)
    def _():
        result((final - 1) % 2, order_ref[jnp.maximum(final - 1, 0)]).wait()

    blanks(lambda copy: copy.wait())


def correlate(left, blocks, labels, me, table):
    order, matched, number, entry = table
    count, subjects, depth, _ = blocks.shape
    _, width, frames = left.shape
    strips = 8 if width % 64 == 0 else 1
    smem = pl.BlockSpec(memory_space=pltpu.SMEM)
    hbm = pl.BlockSpec(memory_space=pl.ANY)
    return pl.pallas_call(
        functools.partial(fisher_kernel, [subjects - again for again in range(3)]),
        in_specs=[smem] * 6 + [hbm, hbm],
        out_specs=hbm,
        scratch_shapes=[
            pltpu.VMEM((subjects, width, frames), jnp.bfloat16),
            pltpu.VMEM((2, 2, subjects, depth, LANES), jnp.bfloat16),
            pltpu.VMEM((subjects, frames, LANES), jnp.bfloat16),
            pltpu.VMEM((width // strips, 2 * width), jnp.float32),
            pltpu.VMEM((2, width, 2 * width), jnp.float32),
            pltpu.SemaphoreType.DMA((count // 2, strips)),
            pltpu.SemaphoreType.DMA((2,)),
            pltpu.SemaphoreType.DMA((2, 2)),
            pltpu.SemaphoreType.DMA,
        ],
        out_shape=jax.ShapeDtypeStruct((width, count * width), jnp.float32),
        compiler_params=pltpu.CompilerParams(vmem_limit_bytes=60 * 1024 * 1024),
        name="correlate",
    )(labels, me, order, matched, number, entry, left, blocks)


def on_device(series, subject_ids, net_labels):
    count = lax.axis_size("blk")
    pool, frames, width = series.shape
    subjects = subject_ids.shape[0]
    packs = width % LANES == HALF and frames % 32 == 0
    fits = net_labels.shape[0] == count and count % 4 == 0 and lax.axis_size("parts") == 2
    if not (packs and fits and pool < 32 and subjects == FORMS[-1][0]):
        return plain(series, subject_ids, net_labels)
    me = lax.axis_index("blk").astype(jnp.int32)[None]
    part = lax.axis_index("parts").astype(jnp.int32)[None]
    others = lax.ppermute(subject_ids, "parts", [(0, 1), (1, 0)])
    listed, form, *table = distinct(pool, subject_ids, others, part, net_labels, me)
    runs = [
        functools.partial(
            gather, count=count, subjects=subjects, held=held, passed=passed, collective_id=i
        )
        for i, (held, passed) in enumerate(FORMS)
    ]
    blocks, left = lax.switch(form[0], runs, listed, series)
    return correlate(left, blocks, net_labels, me, table)


def solution(mesh):
    return jax.shard_map(
        on_device,
        mesh=mesh,
        in_specs=(P(None, None, "blk"), P("parts"), P()),
        out_specs=P(("parts", "blk"), None),
        check_vma=False,
    )
```

```python
import functools

import jax
import jax.numpy as jnp
from jax import lax
from jax.experimental import pallas as pl
from jax.experimental.pallas import tpu as pltpu
from jax.sharding import PartitionSpec as P

LIMIT = 0.999
LANES = 128
HALF = LANES // 2
FORMS = [(4, 1, 1), (4, 2, 0), (5, 2, 0), (5, 2, 1), (6, 2, 0), (8, 0, 0)]


def normalize(chosen):
    values = chosen.astype(jnp.float32)
    center = values - jnp.mean(values, axis=1, keepdims=True)
    spread = jnp.mean(center * center, axis=1, keepdims=True)
    return (center / jnp.sqrt(spread + 1e-05)).astype(jnp.bfloat16)


def fisher_sum(left, right):
    frames = left.shape[1]
    total = jnp.zeros((left.shape[2], right.shape[2]), jnp.float32)
    for subject in range(left.shape[0]):
        corr = (
            lax.dot_general(
                left[subject],
                right[subject],
                (((0,), (0,)), ((), ())),
                preferred_element_type=jnp.float32,
            )
            / frames
        )
        clipped = jnp.clip(corr, -LIMIT, LIMIT)
        total = total + 0.5 * jnp.log((1.0 + clipped) / (1.0 - clipped))
    return total


def plain(series, subject_ids, net_labels):
    normalized = normalize(jnp.take(series, subject_ids, axis=0))
    rows = normalized.shape[2]
    index = lax.axis_index("blk")
    count = lax.axis_size("blk")
    row_labels = jnp.repeat(net_labels, count * rows // net_labels.shape[0])
    own_labels = lax.dynamic_slice_in_dim(row_labels, index * rows, rows)
    gathered = lax.all_gather(normalized, "blk", axis=2, tiled=True)
    same = own_labels[:, None] == row_labels[None, :]
    return jnp.where(same, fisher_sum(normalized, gathered), 0.0)


def plan_kernel(
    pool, mine_ref, theirs_ref, first_ref, labels_ref, me_ref,
    list_ref, form_ref, order_ref, pairs_ref, number_ref, entry_ref,
    where_ref,
):
    subjects = mine_ref.shape[0]
    one, zero = jnp.int32(1), jnp.int32(0)

    def members(ref):
        bits = zero
        for s in range(subjects):
            bits = bits | (one << ref[s])
        return [(bits >> p) & 1 for p in range(pool)]

    mine, theirs = members(mine_ref), members(theirs_ref)
    own, other = sum(mine), sum(theirs)
    both = sum(a * b for a, b in zip(mine, theirs))
    form = jnp.int32(len(FORMS) - 1)
    held, late, split = (jnp.int32(value) for value in FORMS[-1])
    for index in reversed(range(len(FORMS) - 1)):
        carried, passed, halved = FORMS[index]
        lack = jnp.maximum(own - halved - carried, 0)
        give = jnp.maximum(other - halved - carried, 0)
        fits = jnp.logical_and(jnp.maximum(lack, give) <= passed, lack + give + halved <= both)
        form = jnp.where(fits, index, form)
        held = jnp.where(fits, carried, held)
        late = jnp.where(fits, passed, late)
        split = jnp.where(fits, halved, split)
    form_ref[0] = form
    lack, give = jnp.maximum(own - split - held, 0), jnp.maximum(other - split - held, 0)
    first = first_ref[0] == 0
    give_from = jnp.where(first, 0, lack)
    lack_from = jnp.where(first, give, 0)
    for s in range(list_ref.shape[0]):
        list_ref[s] = mine_ref[0]
    rank, plain_at = zero, give
    for p in range(pool):
        common = mine[p] * theirs[p]
        gives = jnp.logical_and(rank >= give_from, rank < give_from + give)
        gives = jnp.logical_and(gives, common == 1)
        lacks = jnp.logical_and(rank >= lack_from, rank < lack_from + lack)
        lacks = jnp.logical_and(lacks, common == 1)
        halves = jnp.logical_and(common * split == 1, rank == lack + give)
        at = jnp.where(gives, rank - give_from, jnp.where(lacks, held + rank - lack_from, plain_at))
        at = jnp.where(halves, held + late, at)
        moved = jnp.logical_or(halves, jnp.logical_or(gives, lacks))
        kept = jnp.logical_and(mine[p] == 1, jnp.logical_not(moved))
        plain_at = plain_at + kept.astype(jnp.int32)
        rank = rank + common
        where_ref[p] = at
        list_ref[jnp.where(mine[p] == 1, at, subjects)] = jnp.int32(p)
    times = [sum((mine_ref[s] == p).astype(jnp.int32) for s in range(subjects)) for p in range(pool)]
    most = times[0]
    for t in times[1:]:
        most = jnp.maximum(most, t)
    squares = jnp.logical_and(most <= 2, own > subjects - 3)
    number_ref[0] = jnp.where(squares, own, subjects)
    for s in range(subjects):
        entry_ref[s] = where_ref[mine_ref[s]]

    @pl.when(squares)
    def _():
        many_at, one_at = zero, sum((t > 1).astype(jnp.int32) for t in times)
        for p in range(pool):
            many, single = times[p] > 1, times[p] == 1
            at = jnp.where(many, many_at, jnp.where(single, one_at, subjects))
            entry_ref[at] = where_ref[p]
            many_at = many_at + many.astype(jnp.int32)
            one_at = one_at + single.astype(jnp.int32)

    label = labels_ref[me_ref[0]]
    pairs = order_ref.shape[0] - 1
    found = zero
    for p in range(pairs):
        front, back = labels_ref[2 * p] == label, labels_ref[2 * p + 1] == label
        hit = jnp.logical_or(front, back)
        at = jnp.where(hit, found, pairs)
        order_ref[at] = jnp.int32(p)
        found = found + hit.astype(jnp.int32)
    pairs_ref[0] = found


def distinct(pool, mine, theirs, part, labels, me):
    subjects = mine.shape[0]
    spots = labels.shape[0] // 2 + 1
    sizes = [subjects + 1, 1, spots, 1, 1, subjects + 1]
    return pl.pallas_call(
        functools.partial(plan_kernel, pool),
        out_shape=[jax.ShapeDtypeStruct((size,), jnp.int32) for size in sizes],
        in_specs=[pl.BlockSpec(memory_space=pltpu.SMEM)] * 5,
        out_specs=[pl.BlockSpec(memory_space=pltpu.SMEM)] * len(sizes),
        scratch_shapes=[pltpu.SMEM((pool,), jnp.int32)],
        name="plan",
    )(mine, theirs, part, labels, me)


def gather_kernel(
    count, pieces, half, form, ids_ref, series_ref, out_ref, left_ref,
    pool, packed, turned, load_sem, store_sem, send_sem, recv_sem,
):
    tall = count // 4
    me = lax.axis_index("blk")
    part = lax.axis_index("parts")
    z = me // 4
    x = (me // 2) % 2
    c = me % 2
    held, passed, split = form
    chunks = len(pieces)
    starts = [start for start, _ in pieces]
    sizes = [size for _, size in pieces]
    apart = held + passed
    total = apart + split
    shares = [
        1 if start == apart and split else max(0, min(passed - start, size))
        for start, size in pieces
    ]
    rows = out_ref.shape[2] // 2
    near = pl.ds(pl.multiple_of(part * rows, 16), rows)
    far = pl.ds(pl.multiple_of((1 - part) * rows, 16), rows)
    UP, DOWN, SIDE, TWIN, OVER, LATE = range(6)

    def device(zz, xx, cc):
        return (zz * 2 + xx) * 2 + cc

    target = {
        UP: {"blk": device(jnp.minimum(z + 1, tall - 1), x, c)},
        DOWN: {"blk": device(jnp.maximum(z - 1, 0), x, c)},
        SIDE: {"blk": device(z, 1 - x, c)},
        TWIN: {"blk": device(z, x, 1 - c)},
        OVER: {"parts": 1 - part},
        LATE: {"blk": device(z, x, 1 - c)},
    }
    has_up, has_down = z + 1 < tall, z > 0

    load = pltpu.make_async_copy(series_ref, pool, load_sem)
    load.start()
    barrier = pltpu.get_barrier_semaphore()

    def greet(way):
        pl.semaphore_signal(
            barrier, inc=1, device_id=target[way], device_id_type=pl.DeviceIdType.MESH
        )

    greet(SIDE)
    greet(TWIN)
    greet(OVER)
    pl.when(has_up)(lambda: greet(UP))
    pl.when(has_down)(lambda: greet(DOWN))
    pl.semaphore_wait(barrier, 3 + has_up.astype(jnp.int32) + has_down.astype(jnp.int32))

    def copy(way, block, q):
        late = int(way in (OVER, LATE))
        if split and starts[q] == apart:
            source = landing = (block, apart, far if way == LATE else near)
        elif late:
            landing = (block, pl.ds(held + starts[q], shares[q]))
            source = landing if way == LATE else (block, pl.ds(starts[q], shares[q]))
        else:
            source = landing = (block, pl.ds(starts[q], sizes[q]))
        return pltpu.make_async_remote_copy(
            src_ref=out_ref.at[source],
            dst_ref=out_ref.at[landing],
            send_sem=send_sem.at[way, block, q],
            recv_sem=recv_sem.at[late, block, q],
            device_id=target[way],
            device_id_type=pl.DeviceIdType.MESH,
        )

    def send(way, block, q):
        copy(way, block, q).start()

    def arrived(block, q):
        copy(TWIN, block, q).wait_recv()

    def by_side(zz, at, q):
        if q < half:
            return jnp.bool_(True)
        low = jnp.logical_and(zz == 0, at > 0)
        high = jnp.logical_and(zz == tall - 1, at < tall - 1)
        return jnp.logical_not(jnp.logical_or(low, high))

    def stores(s):
        slot = s % 2
        return [
            pltpu.make_async_copy(packed.at[slot], out_ref.at[me, s], store_sem.at[0, slot]),
            pltpu.make_async_copy(turned.at[slot], left_ref.at[s], store_sem.at[1, slot]),
        ]

    def normalize(s):
        slot = s % 2
        values = pool[ids_ref[s]].astype(jnp.float32)
        frames, width = values.shape
        center = values - jnp.sum(values, axis=0, keepdims=True) / frames
        spread = jnp.sum(center * center, axis=0, keepdims=True) / frames
        result = (center * (1.0 / jnp.sqrt(spread + 1e-05))).astype(jnp.bfloat16)
        turned[slot] = result.T
        tiles, top = width // LANES, frames // 2

        def pack(first, edge, upper, lower):
            for t in range(tiles):
                start = first + t * LANES
                packed[slot, t * frames : (t + 1) * frames, :] = result[:, start : start + LANES]
            ends = {upper: result[:top, edge : edge + HALF], lower: result[top:, edge : edge + HALF]}
            packed[slot, tiles * frames :, :] = jnp.concatenate([ends[0], ends[1]], axis=1)

        pl.when(c == 0)(lambda: pack(0, tiles * LANES, 0, 1))
        pl.when(c == 1)(lambda: pack(HALF, 0, 1, 0))

    def prepare(s, carry):
        @pl.when(s < total)
        def _():
            normalize(s)
            for copy_out in stores(s):
                copy_out.start()

        @pl.when(s >= 1)
        def _():
            for copy_out in stores(s - 1):
                copy_out.wait()
            for q in range(chunks):
                @pl.when(s == starts[q] + sizes[q])
                def _():
                    pl.when(has_up)(lambda: send(UP, me, q))
                    pl.when(has_down)(lambda: send(DOWN, me, q))
                    pl.when(by_side(z, z, q))(lambda: send(SIDE, me, q))
                    send(TWIN, me, q)

                if shares[q]:
                    ready = total if starts[q] == apart else held + starts[q] + shares[q]
                    pl.when(s == ready)(lambda: send(LATE, me, q))

        return carry

    load.wait()
    lax.fori_loop(0, total + 1, prepare, 0)

    def visit(k, q, act):
        pl.when(z - k >= 0)(lambda: act(device(z - k, x, c), q, "low", k))
        pl.when(z + k < tall)(lambda: act(device(z + k, x, c), q, "high", k))
        if q >= half:
            pl.when(jnp.logical_and(z - k == -1, has_down))(
                lambda: act(device(0, 1 - x, c), q, "bottom", k)
            )
            pl.when(jnp.logical_and(z + k == tall, has_up))(
                lambda: act(device(tall - 1, 1 - x, c), q, "top", k)
            )
        pl.when(k == 1)(lambda: act(device(z, 1 - x, c), q, "side", k))
        low = z - k + 1
        pl.when(jnp.logical_and(jnp.logical_and(k > 1, low >= 0), by_side(low, z, q)))(
            lambda: act(device(low, 1 - x, c), q, "end", k)
        )
        high = z + k - 1
        pl.when(jnp.logical_and(jnp.logical_and(k > 1, high < tall), by_side(high, z, q)))(
            lambda: act(device(high, 1 - x, c), q, "end", k)
        )

    def relay(block, q, kind, k):
        arrived(block, q)
        if kind == "low":
            pl.when(has_up)(lambda: send(UP, block, q))
            pl.when(by_side(z - k, z, q))(lambda: send(SIDE, block, q))
        if kind == "high":
            pl.when(has_down)(lambda: send(DOWN, block, q))
            pl.when(by_side(z + k, z, q))(lambda: send(SIDE, block, q))
        if kind == "bottom":
            pl.when(has_up)(lambda: send(UP, block, q))
        if kind == "top":
            pl.when(has_down)(lambda: send(DOWN, block, q))
        if kind == "side" and q >= half:
            pl.when(jnp.logical_and(z == 0, has_up))(lambda: send(UP, block, q))
            pl.when(jnp.logical_and(z == tall - 1, has_down))(lambda: send(DOWN, block, q))
        send(TWIN, block, q)
        if shares[q]:
            send(OVER, block, q)

    def pass_on(block, q, kind, k):
        copy(OVER, block, q).wait_recv()
        send(LATE, block, q)

    def step(k, carry):
        for q in range(chunks):
            pl.when(k <= tall)(lambda: visit(k, q, relay))
            if shares[q]:
                pl.when(k >= 2)(lambda: visit(k - 1, q, pass_on))
        return carry

    lax.fori_loop(1, tall + (2 if passed + split else 1), step, 0)

    def finish(zz, carry):
        for q in range(chunks):
            own = device(zz, x, c)
            other = device(zz, 1 - x, c)
            arrived(device(zz, x, 1 - c), q)
            arrived(device(zz, 1 - x, 1 - c), q)
            copy(TWIN, own, q).wait_send()
            copy(TWIN, other, q).wait_send()
            pl.when(by_side(zz, z, q))(lambda: copy(SIDE, own, q).wait_send())
            pl.when(jnp.logical_and(has_up, zz <= z))(lambda: copy(UP, own, q).wait_send())
            pl.when(jnp.logical_and(has_down, zz >= z))(lambda: copy(DOWN, own, q).wait_send())
            if q >= half:
                pl.when(jnp.logical_and(has_up, zz == 0))(
                    lambda: copy(UP, other, q).wait_send()
                )
                pl.when(jnp.logical_and(has_down, zz == tall - 1))(
                    lambda: copy(DOWN, other, q).wait_send()
                )
            if shares[q]:
                copy(LATE, device(zz, x, 1 - c), q).wait_recv()
                copy(LATE, device(zz, 1 - x, 1 - c), q).wait_recv()
                copy(LATE, own, q).wait_send()
                copy(LATE, other, q).wait_send()
                pl.when(zz != z)(lambda: copy(OVER, own, q).wait_send())
                copy(OVER, other, q).wait_send()
        return carry

    lax.fori_loop(0, tall, finish, 0)


def chunks_of(held, passed, split):
    early = held - held // 2
    rest, late = early - passed, held // 2
    halves = [[1] * passed + [rest - rest // 2, rest // 2], [late - late // 2, late // 2]]
    pieces, start = [], 0
    for half in halves:
        pieces.append([])
        for size in half:
            if size:
                pieces[-1].append((start, size))
            start += size
    if split:
        pieces[1].insert(0, (held + passed, 1))
    return pieces


def gather(listed, series, count, subjects, form, collective_id):
    early, late = chunks_of(*form)
    pieces = early + late
    pool, frames, width = series.shape
    depth = width * frames // LANES
    return pl.pallas_call(
        functools.partial(gather_kernel, count, pieces, len(early), form),
        out_shape=[
            jax.ShapeDtypeStruct((count, subjects, depth, LANES), jnp.bfloat16),
            jax.ShapeDtypeStruct((subjects, width, frames), jnp.bfloat16),
        ],
        in_specs=[pl.BlockSpec(memory_space=pltpu.SMEM), pl.BlockSpec(memory_space=pl.ANY)],
        out_specs=[pl.BlockSpec(memory_space=pl.ANY)] * 2,
        scratch_shapes=[
            pltpu.VMEM((pool, frames, width), jnp.bfloat16),
            pltpu.VMEM((2, depth, LANES), jnp.bfloat16),
            pltpu.VMEM((2, width, frames), jnp.bfloat16),
            pltpu.SemaphoreType.DMA,
            pltpu.SemaphoreType.DMA((2, 2)),
            pltpu.SemaphoreType.DMA((6, count, len(pieces))),
            pltpu.SemaphoreType.DMA((2, count, len(pieces))),
        ],
        compiler_params=pltpu.CompilerParams(
            collective_id=collective_id, has_side_effects=True
        ),
        name="gather_{}_{}_{}".format(*form),
    )(listed, series)


def fisher_kernel(
    counts, labels_ref, me_ref, order_ref, matched_ref, number_ref, entry_ref,
    source_ref, blocks_ref, out_ref, left_ref, right, middle, zeros, done,
    zero_sem, done_sem, right_sem, left_sem,
):
    subjects, width, frames = left_ref.shape
    pairs = order_ref.shape[0] - 1
    own = labels_ref[me_ref[0]]
    tiles, top = width // LANES, frames // 2
    bound = LIMIT * frames
    strip = zeros.shape[0]
    matched = matched_ref[0]

    def columns(p):
        return pl.ds(pl.multiple_of(p * 2 * width, LANES), 2 * width)

    def blank(p, r):
        target = out_ref.at[r * strip : (r + 1) * strip, columns(p)]
        return pltpu.make_async_copy(zeros, target, zero_sem.at[p, r])

    def result(slot, p):
        return pltpu.make_async_copy(done.at[slot], out_ref.at[:, columns(p)], done_sem.at[slot])

    def empty(p):
        return jnp.logical_not(
            jnp.logical_or(labels_ref[2 * p] == own, labels_ref[2 * p + 1] == own)
        )

    def fetch(step, act):
        slot = step % 2
        for side in range(2):
            block = 2 * order_ref[step] + side

            @pl.when(labels_ref[block] == own)
            def _():
                act(
                    pltpu.make_async_copy(
                        blocks_ref.at[block], right.at[slot, side], right_sem.at[slot, side]
                    )
                )

    whole = pltpu.make_async_copy(source_ref, left_ref, left_sem)
    whole.start()
    fetch(0, lambda copy: copy.start())
    zeros[...] = jnp.zeros_like(zeros)

    def blanks(act):
        for p in range(pairs):
            @pl.when(empty(p))
            def _():
                for r in range(width // strip):
                    act(blank(p, r))

    def body(step, carry):
        spot = order_ref[step]
        first = labels_ref[2 * spot] == own
        second = labels_ref[2 * spot + 1] == own
        now = step % 2
        fetch(step, lambda copy: copy.wait())
        pl.when(step + 1 < matched)(lambda: fetch(step + 1, lambda copy: copy.start()))
        @pl.when(step == 0)
        def _():
            whole.wait()
            blanks(lambda copy: copy.start())

        pl.when(step >= 2)(lambda: result(now, spot).wait())

        for s in range(subjects):
            a = right[now, 0, s, tiles * frames :, :].astype(jnp.float32)
            b = right[now, 1, s, tiles * frames :, :].astype(jnp.float32)
            front = lax.broadcasted_iota(jnp.int32, a.shape, 1) < HALF
            middle[s, :top, :] = jnp.where(front, a, b).astype(jnp.bfloat16)
            swapped = pltpu.roll(jnp.where(front, b, a), HALF, 1)
            middle[s, top:, :] = swapped.astype(jnp.bfloat16)

        def tile(start, size, wanted, mixed, columns_of):
            lanes = pl.ds(start, size)

            def value(count):
                over = under = None
                for s in range(count):
                    slot = entry_ref[s]
                    these = columns_of(slot)
                    dot = jnp.dot(left_ref[slot], these, preferred_element_type=jnp.float32)
                    dot = jnp.clip(dot, -bound, bound)
                    plus, minus = frames + dot, frames - dot
                    if s < subjects - count:
                        plus, minus = plus * plus, minus * minus
                    over = plus if over is None else over * plus
                    under = minus if under is None else under * minus
                return 0.5 * jnp.log(over / under)

            @pl.when(jnp.logical_not(wanted))
            def _():
                done[now, :, lanes] = jnp.zeros((width, size), jnp.float32)

            for count in counts:
                @pl.when(jnp.logical_and(wanted, number_ref[0] == count))
                def _():
                    total = value(count)
                    if mixed:
                        lane = start + lax.broadcasted_iota(jnp.int32, total.shape, 1)
                        keep = jnp.where(
                            lane < width, first.astype(jnp.int32), second.astype(jnp.int32)
                        )
                        total = jnp.where(keep > 0, total, 0.0)
                    done[now, :, lanes] = total

        def stripe(side, slot, row):
            return right[now, side, slot, pl.ds(pl.multiple_of(row * frames, 16), frames), :]

        couples = tiles // 2
        spare = tiles % 2

        def couple(k, carry):
            side = k // couples
            row = 2 * (k % couples) + side * spare
            start = pl.multiple_of((side * (tiles + 1) + row) * LANES, LANES)
            tile(
                start, 2 * LANES, jnp.where(side == 0, first, second), False,
                lambda slot: jnp.concatenate(
                    [stripe(side, slot, row), stripe(side, slot, row + 1)], axis=1
                ),
            )
            return carry

        lax.fori_loop(0, 2 * couples, couple, 0)
        either = jnp.logical_or(first, second)
        if spare:
            tile(
                (tiles - 1) * LANES, 2 * LANES, either, True,
                lambda slot: jnp.concatenate([stripe(0, slot, tiles - 1), middle[slot]], axis=1),
            )
            tile((tiles + 1) * LANES, LANES, second, False, lambda slot: stripe(1, slot, 0))
        else:
            tile(tiles * LANES, LANES, either, True, lambda slot: middle[slot])

        result(now, spot).start()
        return carry

    lax.fori_loop(0, matched, body, 0)
    final = matched - 1
    result(final % 2, order_ref[final]).wait()

    @pl.when(final >= 1)
    def _():
        result((final - 1) % 2, order_ref[jnp.maximum(final - 1, 0)]).wait()

    blanks(lambda copy: copy.wait())


def correlate(left, blocks, labels, me, table):
    order, matched, number, entry = table
    count, subjects, depth, _ = blocks.shape
    _, width, frames = left.shape
    strips = 8 if width % 64 == 0 else 1
    smem = pl.BlockSpec(memory_space=pltpu.SMEM)
    hbm = pl.BlockSpec(memory_space=pl.ANY)
    return pl.pallas_call(
        functools.partial(fisher_kernel, [subjects - again for again in range(3)]),
        in_specs=[smem] * 6 + [hbm, hbm],
        out_specs=hbm,
        scratch_shapes=[
            pltpu.VMEM((subjects, width, frames), jnp.bfloat16),
            pltpu.VMEM((2, 2, subjects, depth, LANES), jnp.bfloat16),
            pltpu.VMEM((subjects, frames, LANES), jnp.bfloat16),
            pltpu.VMEM((width // strips, 2 * width), jnp.float32),
            pltpu.VMEM((2, width, 2 * width), jnp.float32),
            pltpu.SemaphoreType.DMA((count // 2, strips)),
            pltpu.SemaphoreType.DMA((2,)),
            pltpu.SemaphoreType.DMA((2, 2)),
            pltpu.SemaphoreType.DMA,
        ],
        out_shape=jax.ShapeDtypeStruct((width, count * width), jnp.float32),
        compiler_params=pltpu.CompilerParams(vmem_limit_bytes=60 * 1024 * 1024),
        name="correlate",
    )(labels, me, order, matched, number, entry, left, blocks)


def on_device(series, subject_ids, net_labels):
    count = lax.axis_size("blk")
    pool, frames, width = series.shape
    subjects = subject_ids.shape[0]
    packs = width % LANES == HALF and frames % 32 == 0 and width * frames // LANES % 32 == 0
    fits = net_labels.shape[0] == count and count % 4 == 0 and lax.axis_size("parts") == 2
    if not (packs and fits and pool < 32 and subjects == FORMS[-1][0]):
        return plain(series, subject_ids, net_labels)
    me = lax.axis_index("blk").astype(jnp.int32)[None]
    part = lax.axis_index("parts").astype(jnp.int32)[None]
    others = lax.ppermute(subject_ids, "parts", [(0, 1), (1, 0)])
    listed, chosen, *table = distinct(pool, subject_ids, others, part, net_labels, me)
    runs = [
        functools.partial(gather, count=count, subjects=subjects, form=form, collective_id=i)
        for i, form in enumerate(FORMS)
    ]
    blocks, left = lax.switch(chosen[0], runs, listed, series)
    return correlate(left, blocks, net_labels, me, table)


def solution(mesh):
    return jax.shard_map(
        on_device,
        mesh=mesh,
        in_specs=(P(None, None, "blk"), P("parts"), P()),
        out_specs=P(("parts", "blk"), None),
        check_vma=False,
    )
```

```python
import functools

import jax
import jax.numpy as jnp
from jax import lax
from jax.experimental import pallas as pl
from jax.experimental.pallas import tpu as pltpu
from jax.sharding import PartitionSpec as P

LIMIT = 0.999
LANES = 128
HALF = LANES // 2
SQUARES = 3
FORMS = [(4, 1, 1), (4, 2, 0), (5, 2, 0), (5, 2, 1), (6, 2, 0), (8, 0, 0)]


def normalize(chosen):
    values = chosen.astype(jnp.float32)
    center = values - jnp.mean(values, axis=1, keepdims=True)
    spread = jnp.mean(center * center, axis=1, keepdims=True)
    return (center / jnp.sqrt(spread + 1e-05)).astype(jnp.bfloat16)


def fisher_sum(left, right):
    frames = left.shape[1]
    total = jnp.zeros((left.shape[2], right.shape[2]), jnp.float32)
    for subject in range(left.shape[0]):
        corr = (
            lax.dot_general(
                left[subject],
                right[subject],
                (((0,), (0,)), ((), ())),
                preferred_element_type=jnp.float32,
            )
            / frames
        )
        clipped = jnp.clip(corr, -LIMIT, LIMIT)
        total = total + 0.5 * jnp.log((1.0 + clipped) / (1.0 - clipped))
    return total


def plain(series, subject_ids, net_labels):
    normalized = normalize(jnp.take(series, subject_ids, axis=0))
    rows = normalized.shape[2]
    index = lax.axis_index("blk")
    count = lax.axis_size("blk")
    row_labels = jnp.repeat(net_labels, count * rows // net_labels.shape[0])
    own_labels = lax.dynamic_slice_in_dim(row_labels, index * rows, rows)
    gathered = lax.all_gather(normalized, "blk", axis=2, tiled=True)
    same = own_labels[:, None] == row_labels[None, :]
    return jnp.where(same, fisher_sum(normalized, gathered), 0.0)


def plan_kernel(
    pool, mine_ref, theirs_ref, first_ref, labels_ref, me_ref,
    list_ref, form_ref, order_ref, pairs_ref, number_ref, entry_ref,
    where_ref, pair_ref,
):
    subjects = mine_ref.shape[0]
    one, zero = jnp.int32(1), jnp.int32(0)

    def members(ref):
        bits = zero
        for s in range(subjects):
            bits = bits | (one << ref[s])
        return [(bits >> p) & 1 for p in range(pool)]

    mine, theirs = members(mine_ref), members(theirs_ref)
    own, other = sum(mine), sum(theirs)
    both = sum(a * b for a, b in zip(mine, theirs))
    form = jnp.int32(len(FORMS) - 1)
    held, late, split = (jnp.int32(value) for value in FORMS[-1])
    for index in reversed(range(len(FORMS) - 1)):
        carried, passed, halved = FORMS[index]
        lack = jnp.maximum(own - halved - carried, 0)
        give = jnp.maximum(other - halved - carried, 0)
        fits = jnp.logical_and(jnp.maximum(lack, give) <= passed, lack + give + halved <= both)
        form = jnp.where(fits, index, form)
        held = jnp.where(fits, carried, held)
        late = jnp.where(fits, passed, late)
        split = jnp.where(fits, halved, split)
    form_ref[0] = form
    lack, give = jnp.maximum(own - split - held, 0), jnp.maximum(other - split - held, 0)
    first = first_ref[0] == 0
    give_from = jnp.where(first, 0, lack)
    lack_from = jnp.where(first, give, 0)
    for s in range(list_ref.shape[0]):
        list_ref[s] = mine_ref[0]
    rank, plain_at = zero, give
    for p in range(pool):
        common = mine[p] * theirs[p]
        gives = jnp.logical_and(rank >= give_from, rank < give_from + give)
        gives = jnp.logical_and(gives, common == 1)
        lacks = jnp.logical_and(rank >= lack_from, rank < lack_from + lack)
        lacks = jnp.logical_and(lacks, common == 1)
        halves = jnp.logical_and(common * split == 1, rank == lack + give)
        at = jnp.where(gives, rank - give_from, jnp.where(lacks, held + rank - lack_from, plain_at))
        at = jnp.where(halves, held + late, at)
        moved = jnp.logical_or(halves, jnp.logical_or(gives, lacks))
        kept = jnp.logical_and(mine[p] == 1, jnp.logical_not(moved))
        plain_at = plain_at + kept.astype(jnp.int32)
        rank = rank + common
        where_ref[p] = at
        list_ref[jnp.where(mine[p] == 1, at, subjects)] = jnp.int32(p)
    ids = [mine_ref[s] for s in range(subjects)]
    doubles, singles, taken = [], [], zero
    for s in range(subjects):
        same = [(ids[r] == ids[s]).astype(jnp.int32) for r in range(subjects)]
        before, times = sum(same[:s], zero), sum(same)
        opens = before % 2 == 0
        double = jnp.logical_and(opens, times > before + 1)
        double = jnp.logical_and(double, taken < SQUARES).astype(jnp.int32)
        taken = taken + double
        closes = jnp.where(opens, 0, pair_ref[ids[s]])
        pair_ref[ids[s]] = double
        doubles.append(double)
        singles.append(1 - double - closes)
    number_ref[0] = subjects - taken
    many_at, one_at = zero, taken
    for s in range(subjects):
        at = jnp.where(doubles[s] == 1, many_at, jnp.where(singles[s] == 1, one_at, subjects))
        entry_ref[at] = where_ref[ids[s]]
        many_at, one_at = many_at + doubles[s], one_at + singles[s]

    label = labels_ref[me_ref[0]]
    pairs = order_ref.shape[0] - 1
    found = zero
    for p in range(pairs):
        front, back = labels_ref[2 * p] == label, labels_ref[2 * p + 1] == label
        hit = jnp.logical_or(front, back)
        at = jnp.where(hit, found, pairs)
        order_ref[at] = jnp.int32(p)
        found = found + hit.astype(jnp.int32)
    pairs_ref[0] = found


def distinct(pool, mine, theirs, part, labels, me):
    subjects = mine.shape[0]
    spots = labels.shape[0] // 2 + 1
    sizes = [subjects + 1, 1, spots, 1, 1, subjects + 1]
    return pl.pallas_call(
        functools.partial(plan_kernel, pool),
        out_shape=[jax.ShapeDtypeStruct((size,), jnp.int32) for size in sizes],
        in_specs=[pl.BlockSpec(memory_space=pltpu.SMEM)] * 5,
        out_specs=[pl.BlockSpec(memory_space=pltpu.SMEM)] * len(sizes),
        scratch_shapes=[pltpu.SMEM((pool,), jnp.int32)] * 2,
        name="plan",
    )(mine, theirs, part, labels, me)


def gather_kernel(
    count, pieces, half, form, ids_ref, series_ref, out_ref, left_ref,
    pool, packed, turned, load_sem, store_sem, send_sem, recv_sem,
):
    tall = count // 4
    me = lax.axis_index("blk")
    part = lax.axis_index("parts")
    z = me // 4
    x = (me // 2) % 2
    c = me % 2
    held, passed, split = form
    chunks = len(pieces)
    starts = [start for start, _, _ in pieces]
    sizes = [size for _, size, _ in pieces]
    apart = held + passed
    total = apart + split
    shares = [
        1 if start == apart and split else max(0, min(passed - start, size))
        for start, size, _ in pieces
    ]
    rows = out_ref.shape[2] // 2
    near = pl.ds(pl.multiple_of(part * rows, 16), rows)
    far = pl.ds(pl.multiple_of((1 - part) * rows, 16), rows)
    UP, DOWN, SIDE, TWIN, OVER, LATE = range(6)

    def device(zz, xx, cc):
        return (zz * 2 + xx) * 2 + cc

    target = {
        UP: {"blk": device(jnp.minimum(z + 1, tall - 1), x, c)},
        DOWN: {"blk": device(jnp.maximum(z - 1, 0), x, c)},
        SIDE: {"blk": device(z, 1 - x, c)},
        TWIN: {"blk": device(z, x, 1 - c)},
        OVER: {"parts": 1 - part},
        LATE: {"blk": device(z, x, 1 - c)},
    }
    has_up, has_down = z + 1 < tall, z > 0

    load = pltpu.make_async_copy(series_ref, pool, load_sem)
    load.start()
    barrier = pltpu.get_barrier_semaphore()

    def greet(way):
        pl.semaphore_signal(
            barrier, inc=1, device_id=target[way], device_id_type=pl.DeviceIdType.MESH
        )

    greet(SIDE)
    greet(TWIN)
    greet(OVER)
    pl.when(has_up)(lambda: greet(UP))
    pl.when(has_down)(lambda: greet(DOWN))
    pl.semaphore_wait(barrier, 3 + has_up.astype(jnp.int32) + has_down.astype(jnp.int32))

    def copy(way, block, q):
        late = int(way in (OVER, LATE))
        if split and starts[q] == apart:
            source = landing = (block, apart, far if way == LATE else near)
        elif late:
            landing = (block, pl.ds(held + starts[q], shares[q]))
            source = landing if way == LATE else (block, pl.ds(starts[q], shares[q]))
        elif pieces[q][2] is not None:
            source = landing = (block, starts[q], pl.ds(pieces[q][2] * rows, rows))
        else:
            source = landing = (block, pl.ds(starts[q], sizes[q]))
        return pltpu.make_async_remote_copy(
            src_ref=out_ref.at[source],
            dst_ref=out_ref.at[landing],
            send_sem=send_sem.at[way, block, q],
            recv_sem=recv_sem.at[late, block, q],
            device_id=target[way],
            device_id_type=pl.DeviceIdType.MESH,
        )

    def send(way, block, q):
        copy(way, block, q).start()

    def arrived(block, q):
        copy(TWIN, block, q).wait_recv()

    def by_side(zz, at, q):
        if q < half:
            return jnp.bool_(True)
        low = jnp.logical_and(zz == 0, at > 0)
        high = jnp.logical_and(zz == tall - 1, at < tall - 1)
        return jnp.logical_not(jnp.logical_or(low, high))

    def stores(s):
        slot = s % 2
        return [
            pltpu.make_async_copy(packed.at[slot], out_ref.at[me, s], store_sem.at[0, slot]),
            pltpu.make_async_copy(turned.at[slot], left_ref.at[s], store_sem.at[1, slot]),
        ]

    def normalize(s):
        slot = s % 2
        values = pool[ids_ref[s]].astype(jnp.float32)
        frames, width = values.shape
        center = values - jnp.sum(values, axis=0, keepdims=True) / frames
        spread = jnp.sum(center * center, axis=0, keepdims=True) / frames
        result = (center * (1.0 / jnp.sqrt(spread + 1e-05))).astype(jnp.bfloat16)
        turned[slot] = result.T
        tiles, top = width // LANES, frames // 2

        def pack(first, edge, upper, lower):
            for t in range(tiles):
                start = first + t * LANES
                packed[slot, t * frames : (t + 1) * frames, :] = result[:, start : start + LANES]
            ends = {upper: result[:top, edge : edge + HALF], lower: result[top:, edge : edge + HALF]}
            packed[slot, tiles * frames :, :] = jnp.concatenate([ends[0], ends[1]], axis=1)

        pl.when(c == 0)(lambda: pack(0, tiles * LANES, 0, 1))
        pl.when(c == 1)(lambda: pack(HALF, 0, 1, 0))

    def prepare(s, carry):
        @pl.when(s < total)
        def _():
            normalize(s)
            for copy_out in stores(s):
                copy_out.start()

        @pl.when(s >= 1)
        def _():
            for copy_out in stores(s - 1):
                copy_out.wait()
            for q in range(chunks):
                @pl.when(s == starts[q] + sizes[q])
                def _():
                    pl.when(has_up)(lambda: send(UP, me, q))
                    pl.when(has_down)(lambda: send(DOWN, me, q))
                    pl.when(by_side(z, z, q))(lambda: send(SIDE, me, q))
                    send(TWIN, me, q)

                if shares[q]:
                    ready = total if starts[q] == apart else held + starts[q] + shares[q]
                    pl.when(s == ready)(lambda: send(LATE, me, q))

        return carry

    load.wait()
    lax.fori_loop(0, total + 1, prepare, 0)

    def visit(k, q, act):
        pl.when(z - k >= 0)(lambda: act(device(z - k, x, c), q, "low", k))
        pl.when(z + k < tall)(lambda: act(device(z + k, x, c), q, "high", k))
        if q >= half:
            pl.when(jnp.logical_and(z - k == -1, has_down))(
                lambda: act(device(0, 1 - x, c), q, "bottom", k)
            )
            pl.when(jnp.logical_and(z + k == tall, has_up))(
                lambda: act(device(tall - 1, 1 - x, c), q, "top", k)
            )
        pl.when(k == 1)(lambda: act(device(z, 1 - x, c), q, "side", k))
        low = z - k + 1
        pl.when(jnp.logical_and(jnp.logical_and(k > 1, low >= 0), by_side(low, z, q)))(
            lambda: act(device(low, 1 - x, c), q, "end", k)
        )
        high = z + k - 1
        pl.when(jnp.logical_and(jnp.logical_and(k > 1, high < tall), by_side(high, z, q)))(
            lambda: act(device(high, 1 - x, c), q, "end", k)
        )

    def relay(block, q, kind, k):
        arrived(block, q)
        if kind == "low":
            pl.when(has_up)(lambda: send(UP, block, q))
            pl.when(by_side(z - k, z, q))(lambda: send(SIDE, block, q))
        if kind == "high":
            pl.when(has_down)(lambda: send(DOWN, block, q))
            pl.when(by_side(z + k, z, q))(lambda: send(SIDE, block, q))
        if kind == "bottom":
            pl.when(has_up)(lambda: send(UP, block, q))
        if kind == "top":
            pl.when(has_down)(lambda: send(DOWN, block, q))
        if kind == "side" and q >= half:
            pl.when(jnp.logical_and(z == 0, has_up))(lambda: send(UP, block, q))
            pl.when(jnp.logical_and(z == tall - 1, has_down))(lambda: send(DOWN, block, q))
        send(TWIN, block, q)
        if shares[q]:
            send(OVER, block, q)

    def pass_on(block, q, kind, k):
        copy(OVER, block, q).wait_recv()
        send(LATE, block, q)

    def step(k, carry):
        for q in range(chunks):
            pl.when(k <= tall)(lambda: visit(k, q, relay))
            if shares[q]:
                pl.when(k >= 2)(lambda: visit(k - 1, q, pass_on))
        return carry

    lax.fori_loop(1, tall + (2 if passed + split else 1), step, 0)

    def finish(zz, carry):
        for q in range(chunks):
            own = device(zz, x, c)
            other = device(zz, 1 - x, c)
            arrived(device(zz, x, 1 - c), q)
            arrived(device(zz, 1 - x, 1 - c), q)
            copy(TWIN, own, q).wait_send()
            copy(TWIN, other, q).wait_send()
            pl.when(by_side(zz, z, q))(lambda: copy(SIDE, own, q).wait_send())
            pl.when(jnp.logical_and(has_up, zz <= z))(lambda: copy(UP, own, q).wait_send())
            pl.when(jnp.logical_and(has_down, zz >= z))(lambda: copy(DOWN, own, q).wait_send())
            if q >= half:
                pl.when(jnp.logical_and(has_up, zz == 0))(
                    lambda: copy(UP, other, q).wait_send()
                )
                pl.when(jnp.logical_and(has_down, zz == tall - 1))(
                    lambda: copy(DOWN, other, q).wait_send()
                )
            if shares[q]:
                copy(LATE, device(zz, x, 1 - c), q).wait_recv()
                copy(LATE, device(zz, 1 - x, 1 - c), q).wait_recv()
                copy(LATE, own, q).wait_send()
                copy(LATE, other, q).wait_send()
                pl.when(zz != z)(lambda: copy(OVER, own, q).wait_send())
                copy(OVER, other, q).wait_send()
        return carry

    lax.fori_loop(0, tall, finish, 0)


def chunks_of(held, passed, split):
    late = held // 2
    cut = held % 2 if not split and held - late > passed else 0
    rest = held - late - passed - cut
    early_sizes = [1] * passed + [rest - rest // 2, rest // 2]
    late_sizes = [late - late // 2, late // 2]
    halves, start = [[], []], 0
    for half, sizes in zip(halves, [early_sizes, late_sizes]):
        for size in sizes:
            if size:
                half.append((start, size, None))
            start += size
        if half is halves[0] and cut:
            half.append((start, 1, 0))
            halves[1].append((start, 1, 1))
            start += 1
    if split:
        halves[1].insert(0, (held + passed, 1, None))
    return halves


def gather(listed, series, count, subjects, form, collective_id):
    early, late = chunks_of(*form)
    pieces = early + late
    pool, frames, width = series.shape
    depth = width * frames // LANES
    return pl.pallas_call(
        functools.partial(gather_kernel, count, pieces, len(early), form),
        out_shape=[
            jax.ShapeDtypeStruct((count, subjects, depth, LANES), jnp.bfloat16),
            jax.ShapeDtypeStruct((subjects, width, frames), jnp.bfloat16),
        ],
        in_specs=[pl.BlockSpec(memory_space=pltpu.SMEM), pl.BlockSpec(memory_space=pl.ANY)],
        out_specs=[pl.BlockSpec(memory_space=pl.ANY)] * 2,
        scratch_shapes=[
            pltpu.VMEM((pool, frames, width), jnp.bfloat16),
            pltpu.VMEM((2, depth, LANES), jnp.bfloat16),
            pltpu.VMEM((2, width, frames), jnp.bfloat16),
            pltpu.SemaphoreType.DMA,
            pltpu.SemaphoreType.DMA((2, 2)),
            pltpu.SemaphoreType.DMA((6, count, len(pieces))),
            pltpu.SemaphoreType.DMA((2, count, len(pieces))),
        ],
        compiler_params=pltpu.CompilerParams(
            collective_id=collective_id, has_side_effects=True
        ),
        name="gather_{}_{}_{}".format(*form),
    )(listed, series)


def fisher_kernel(
    counts, labels_ref, me_ref, order_ref, matched_ref, number_ref, entry_ref,
    source_ref, blocks_ref, out_ref, left_ref, right, middle, zeros, done,
    zero_sem, done_sem, right_sem, left_sem,
):
    subjects, width, frames = left_ref.shape
    pairs = order_ref.shape[0] - 1
    own = labels_ref[me_ref[0]]
    tiles, top = width // LANES, frames // 2
    bound = LIMIT * frames
    strip = zeros.shape[0]
    matched = matched_ref[0]

    def columns(p):
        return pl.ds(pl.multiple_of(p * 2 * width, LANES), 2 * width)

    def blank(p, r):
        target = out_ref.at[r * strip : (r + 1) * strip, columns(p)]
        return pltpu.make_async_copy(zeros, target, zero_sem.at[p, r])

    def result(slot, p):
        return pltpu.make_async_copy(done.at[slot], out_ref.at[:, columns(p)], done_sem.at[slot])

    def empty(p):
        return jnp.logical_not(
            jnp.logical_or(labels_ref[2 * p] == own, labels_ref[2 * p + 1] == own)
        )

    def fetch(step, act):
        slot = step % 2
        for side in range(2):
            block = 2 * order_ref[step] + side

            @pl.when(labels_ref[block] == own)
            def _():
                act(
                    pltpu.make_async_copy(
                        blocks_ref.at[block], right.at[slot, side], right_sem.at[slot, side]
                    )
                )

    whole = pltpu.make_async_copy(source_ref, left_ref, left_sem)
    whole.start()
    fetch(0, lambda copy: copy.start())
    zeros[...] = jnp.zeros_like(zeros)

    def blanks(act):
        for p in range(pairs):
            @pl.when(empty(p))
            def _():
                for r in range(width // strip):
                    act(blank(p, r))

    def body(step, carry):
        spot = order_ref[step]
        first = labels_ref[2 * spot] == own
        second = labels_ref[2 * spot + 1] == own
        now = step % 2
        fetch(step, lambda copy: copy.wait())
        pl.when(step + 1 < matched)(lambda: fetch(step + 1, lambda copy: copy.start()))
        @pl.when(step == 0)
        def _():
            whole.wait()
            blanks(lambda copy: copy.start())

        pl.when(step >= 2)(lambda: result(now, spot).wait())

        for s in range(subjects):
            a = right[now, 0, s, tiles * frames :, :].astype(jnp.float32)
            b = right[now, 1, s, tiles * frames :, :].astype(jnp.float32)
            front = lax.broadcasted_iota(jnp.int32, a.shape, 1) < HALF
            middle[s, :top, :] = jnp.where(front, a, b).astype(jnp.bfloat16)
            swapped = pltpu.roll(jnp.where(front, b, a), HALF, 1)
            middle[s, top:, :] = swapped.astype(jnp.bfloat16)

        def tile(start, size, wanted, mixed, columns_of):
            lanes = pl.ds(start, size)

            def value(count):
                over = under = None
                for s in range(count):
                    slot = entry_ref[s]
                    these = columns_of(slot)
                    dot = jnp.dot(left_ref[slot], these, preferred_element_type=jnp.float32)
                    dot = jnp.clip(dot, -bound, bound)
                    plus, minus = frames + dot, frames - dot
                    if s < subjects - count:
                        plus, minus = plus * plus, minus * minus
                    over = plus if over is None else over * plus
                    under = minus if under is None else under * minus
                return 0.5 * jnp.log(over / under)

            @pl.when(jnp.logical_not(wanted))
            def _():
                done[now, :, lanes] = jnp.zeros((width, size), jnp.float32)

            for count in counts:
                @pl.when(jnp.logical_and(wanted, number_ref[0] == count))
                def _():
                    total = value(count)
                    if mixed:
                        lane = start + lax.broadcasted_iota(jnp.int32, total.shape, 1)
                        keep = jnp.where(
                            lane < width, first.astype(jnp.int32), second.astype(jnp.int32)
                        )
                        total = jnp.where(keep > 0, total, 0.0)
                    done[now, :, lanes] = total

        def stripe(side, slot, row):
            return right[now, side, slot, pl.ds(pl.multiple_of(row * frames, 16), frames), :]

        couples = tiles // 2
        spare = tiles % 2

        def couple(k, carry):
            side = k // couples
            row = 2 * (k % couples) + side * spare
            start = pl.multiple_of((side * (tiles + 1) + row) * LANES, LANES)
            tile(
                start, 2 * LANES, jnp.where(side == 0, first, second), False,
                lambda slot: jnp.concatenate(
                    [stripe(side, slot, row), stripe(side, slot, row + 1)], axis=1
                ),
            )
            return carry

        lax.fori_loop(0, 2 * couples, couple, 0)
        either = jnp.logical_or(first, second)
        if spare:
            tile(
                (tiles - 1) * LANES, 2 * LANES, either, True,
                lambda slot: jnp.concatenate([stripe(0, slot, tiles - 1), middle[slot]], axis=1),
            )
            tile((tiles + 1) * LANES, LANES, second, False, lambda slot: stripe(1, slot, 0))
        else:
            tile(tiles * LANES, LANES, either, True, lambda slot: middle[slot])

        result(now, spot).start()
        return carry

    lax.fori_loop(0, matched, body, 0)
    final = matched - 1
    result(final % 2, order_ref[final]).wait()

    @pl.when(final >= 1)
    def _():
        result((final - 1) % 2, order_ref[jnp.maximum(final - 1, 0)]).wait()

    blanks(lambda copy: copy.wait())


def correlate(left, blocks, labels, me, table):
    order, matched, number, entry = table
    count, subjects, depth, _ = blocks.shape
    _, width, frames = left.shape
    strips = 8 if width % 64 == 0 else 1
    smem = pl.BlockSpec(memory_space=pltpu.SMEM)
    hbm = pl.BlockSpec(memory_space=pl.ANY)
    return pl.pallas_call(
        functools.partial(fisher_kernel, [subjects - again for again in range(SQUARES + 1)]),
        in_specs=[smem] * 6 + [hbm, hbm],
        out_specs=hbm,
        scratch_shapes=[
            pltpu.VMEM((subjects, width, frames), jnp.bfloat16),
            pltpu.VMEM((2, 2, subjects, depth, LANES), jnp.bfloat16),
            pltpu.VMEM((subjects, frames, LANES), jnp.bfloat16),
            pltpu.VMEM((width // strips, 2 * width), jnp.float32),
            pltpu.VMEM((2, width, 2 * width), jnp.float32),
            pltpu.SemaphoreType.DMA((count // 2, strips)),
            pltpu.SemaphoreType.DMA((2,)),
            pltpu.SemaphoreType.DMA((2, 2)),
            pltpu.SemaphoreType.DMA,
        ],
        out_shape=jax.ShapeDtypeStruct((width, count * width), jnp.float32),
        compiler_params=pltpu.CompilerParams(
            vmem_limit_bytes=60 * 1024 * 1024
        ),
        name="correlate",
    )(labels, me, order, matched, number, entry, left, blocks)


def on_device(series, subject_ids, net_labels):
    count = lax.axis_size("blk")
    pool, frames, width = series.shape
    subjects = subject_ids.shape[0]
    packs = width % LANES == HALF and frames % 32 == 0 and width * frames // LANES % 32 == 0
    fits = net_labels.shape[0] == count and count % 4 == 0 and lax.axis_size("parts") == 2
    if not (packs and fits and pool < 32 and subjects == FORMS[-1][0]):
        return plain(series, subject_ids, net_labels)
    me = lax.axis_index("blk").astype(jnp.int32)[None]
    part = lax.axis_index("parts").astype(jnp.int32)[None]
    others = lax.ppermute(subject_ids, "parts", [(0, 1), (1, 0)])
    listed, chosen, *table = distinct(pool, subject_ids, others, part, net_labels, me)
    runs = [
        functools.partial(gather, count=count, subjects=subjects, form=form, collective_id=i)
        for i, form in enumerate(FORMS)
    ]
    blocks, left = lax.switch(chosen[0], runs, listed, series)
    return correlate(left, blocks, net_labels, me, table)


def solution(mesh):
    return jax.shard_map(
        on_device,
        mesh=mesh,
        in_specs=(P(None, None, "blk"), P("parts"), P()),
        out_specs=P(("parts", "blk"), None),
        check_vma=False,
    )
```

```python
import functools

import jax
import jax.numpy as jnp
from jax import lax
from jax.experimental import pallas as pl
from jax.experimental.pallas import tpu as pltpu
from jax.sharding import PartitionSpec as P

LIMIT = 0.999
LANES = 128
HALF = LANES // 2
SQUARES = 3
FORMS = [(4, 1, 1), (4, 2, 0), (5, 2, 0), (5, 2, 1), (6, 2, 0), (8, 0, 0)]


def normalize(chosen):
    values = chosen.astype(jnp.float32)
    center = values - jnp.mean(values, axis=1, keepdims=True)
    spread = jnp.mean(center * center, axis=1, keepdims=True)
    return (center / jnp.sqrt(spread + 1e-05)).astype(jnp.bfloat16)


def fisher_sum(left, right):
    frames = left.shape[1]
    total = jnp.zeros((left.shape[2], right.shape[2]), jnp.float32)
    for subject in range(left.shape[0]):
        corr = (
            lax.dot_general(
                left[subject],
                right[subject],
                (((0,), (0,)), ((), ())),
                preferred_element_type=jnp.float32,
            )
            / frames
        )
        clipped = jnp.clip(corr, -LIMIT, LIMIT)
        total = total + 0.5 * jnp.log((1.0 + clipped) / (1.0 - clipped))
    return total


def plain(series, subject_ids, net_labels):
    normalized = normalize(jnp.take(series, subject_ids, axis=0))
    rows = normalized.shape[2]
    index = lax.axis_index("blk")
    count = lax.axis_size("blk")
    row_labels = jnp.repeat(net_labels, count * rows // net_labels.shape[0])
    own_labels = lax.dynamic_slice_in_dim(row_labels, index * rows, rows)
    gathered = lax.all_gather(normalized, "blk", axis=2, tiled=True)
    same = own_labels[:, None] == row_labels[None, :]
    return jnp.where(same, fisher_sum(normalized, gathered), 0.0)


def plan_kernel(
    pool, mine_ref, theirs_ref, first_ref, labels_ref, me_ref,
    list_ref, form_ref, order_ref, pairs_ref, number_ref, entry_ref,
    where_ref, pair_ref,
):
    subjects = mine_ref.shape[0]
    one, zero = jnp.int32(1), jnp.int32(0)

    def members(ref):
        bits = zero
        for s in range(subjects):
            bits = bits | (one << ref[s])
        return [(bits >> p) & 1 for p in range(pool)]

    mine, theirs = members(mine_ref), members(theirs_ref)
    own, other = sum(mine), sum(theirs)
    both = sum(a * b for a, b in zip(mine, theirs))
    form = jnp.int32(len(FORMS) - 1)
    held, late, split = (jnp.int32(value) for value in FORMS[-1])
    for index in reversed(range(len(FORMS) - 1)):
        carried, passed, halved = FORMS[index]
        lack = jnp.maximum(own - halved - carried, 0)
        give = jnp.maximum(other - halved - carried, 0)
        fits = jnp.logical_and(jnp.maximum(lack, give) <= passed, lack + give + halved <= both)
        form = jnp.where(fits, index, form)
        held = jnp.where(fits, carried, held)
        late = jnp.where(fits, passed, late)
        split = jnp.where(fits, halved, split)
    form_ref[0] = form
    lack, give = jnp.maximum(own - split - held, 0), jnp.maximum(other - split - held, 0)
    first = first_ref[0] == 0
    give_from = jnp.where(first, 0, lack)
    lack_from = jnp.where(first, give, 0)
    for s in range(list_ref.shape[0]):
        list_ref[s] = mine_ref[0]
    rank, plain_at = zero, give
    for p in range(pool):
        common = mine[p] * theirs[p]
        gives = jnp.logical_and(rank >= give_from, rank < give_from + give)
        gives = jnp.logical_and(gives, common == 1)
        lacks = jnp.logical_and(rank >= lack_from, rank < lack_from + lack)
        lacks = jnp.logical_and(lacks, common == 1)
        halves = jnp.logical_and(common * split == 1, rank == lack + give)
        at = jnp.where(gives, rank - give_from, jnp.where(lacks, held + rank - lack_from, plain_at))
        at = jnp.where(halves, held + late, at)
        moved = jnp.logical_or(halves, jnp.logical_or(gives, lacks))
        kept = jnp.logical_and(mine[p] == 1, jnp.logical_not(moved))
        plain_at = plain_at + kept.astype(jnp.int32)
        rank = rank + common
        where_ref[p] = at
        list_ref[jnp.where(mine[p] == 1, at, subjects)] = jnp.int32(p)
    ids = [mine_ref[s] for s in range(subjects)]
    doubles, singles, taken = [], [], zero
    for s in range(subjects):
        same = [(ids[r] == ids[s]).astype(jnp.int32) for r in range(subjects)]
        before, times = sum(same[:s], zero), sum(same)
        opens = before % 2 == 0
        double = jnp.logical_and(opens, times > before + 1)
        double = jnp.logical_and(double, taken < SQUARES).astype(jnp.int32)
        taken = taken + double
        closes = jnp.where(opens, 0, pair_ref[ids[s]])
        pair_ref[ids[s]] = double
        doubles.append(double)
        singles.append(1 - double - closes)
    number_ref[0] = subjects - taken
    many_at, one_at = zero, taken
    for s in range(subjects):
        at = jnp.where(doubles[s] == 1, many_at, jnp.where(singles[s] == 1, one_at, subjects))
        entry_ref[at] = where_ref[ids[s]]
        many_at, one_at = many_at + doubles[s], one_at + singles[s]

    label = labels_ref[me_ref[0]]
    pairs = order_ref.shape[0] - 1
    found = zero
    for p in range(pairs):
        front, back = labels_ref[2 * p] == label, labels_ref[2 * p + 1] == label
        hit = jnp.logical_or(front, back)
        at = jnp.where(hit, found, pairs)
        order_ref[at] = jnp.int32(p)
        found = found + hit.astype(jnp.int32)
    pairs_ref[0] = found


def distinct(pool, mine, theirs, part, labels, me):
    subjects = mine.shape[0]
    spots = labels.shape[0] // 2 + 1
    sizes = [subjects + 1, 1, spots, 1, 1, subjects + 1]
    return pl.pallas_call(
        functools.partial(plan_kernel, pool),
        out_shape=[jax.ShapeDtypeStruct((size,), jnp.int32) for size in sizes],
        in_specs=[pl.BlockSpec(memory_space=pltpu.SMEM)] * 5,
        out_specs=[pl.BlockSpec(memory_space=pltpu.SMEM)] * len(sizes),
        scratch_shapes=[pltpu.SMEM((pool,), jnp.int32)] * 2,
        name="plan",
    )(mine, theirs, part, labels, me)


def gather_kernel(
    count, pieces, half, form, ids_ref, series_ref, out_ref, left_ref,
    pool, packed, turned, load_sem, store_sem, send_sem, recv_sem,
):
    tall = count // 4
    me = lax.axis_index("blk")
    part = lax.axis_index("parts")
    z = me // 4
    x = (me // 2) % 2
    c = me % 2
    held, passed, split = form
    chunks = len(pieces)
    starts = [start for start, _ in pieces]
    sizes = [size for _, size in pieces]
    apart = held + passed
    total = apart + split
    shares = [
        1 if start == apart and split else max(0, min(passed - start, size))
        for start, size in pieces
    ]
    rows = out_ref.shape[2] // 2
    near = pl.ds(pl.multiple_of(part * rows, 16), rows)
    far = pl.ds(pl.multiple_of((1 - part) * rows, 16), rows)
    UP, DOWN, SIDE, TWIN, OVER, LATE = range(6)

    def device(zz, xx, cc):
        return (zz * 2 + xx) * 2 + cc

    target = {
        UP: {"blk": device(jnp.minimum(z + 1, tall - 1), x, c)},
        DOWN: {"blk": device(jnp.maximum(z - 1, 0), x, c)},
        SIDE: {"blk": device(z, 1 - x, c)},
        TWIN: {"blk": device(z, x, 1 - c)},
        OVER: {"parts": 1 - part},
        LATE: {"blk": device(z, x, 1 - c)},
    }
    has_up, has_down = z + 1 < tall, z > 0

    load = pltpu.make_async_copy(series_ref, pool, load_sem)
    load.start()
    barrier = pltpu.get_barrier_semaphore()

    def greet(way):
        pl.semaphore_signal(
            barrier, inc=1, device_id=target[way], device_id_type=pl.DeviceIdType.MESH
        )

    greet(SIDE)
    greet(TWIN)
    greet(OVER)
    pl.when(has_up)(lambda: greet(UP))
    pl.when(has_down)(lambda: greet(DOWN))
    pl.semaphore_wait(barrier, 3 + has_up.astype(jnp.int32) + has_down.astype(jnp.int32))

    def copy(way, block, q):
        late = int(way in (OVER, LATE))
        if split and starts[q] == apart:
            source = landing = (block, apart, far if way == LATE else near)
        elif late:
            landing = (block, pl.ds(held + starts[q], shares[q]))
            source = landing if way == LATE else (block, pl.ds(starts[q], shares[q]))
        else:
            source = landing = (block, pl.ds(starts[q], sizes[q]))
        return pltpu.make_async_remote_copy(
            src_ref=out_ref.at[source],
            dst_ref=out_ref.at[landing],
            send_sem=send_sem.at[way, block, q],
            recv_sem=recv_sem.at[late, block, q],
            device_id=target[way],
            device_id_type=pl.DeviceIdType.MESH,
        )

    def send(way, block, q):
        copy(way, block, q).start()

    def arrived(block, q):
        copy(TWIN, block, q).wait_recv()

    def by_side(zz, at, q):
        if q < half:
            return jnp.bool_(True)
        low = jnp.logical_and(zz == 0, at > 0)
        high = jnp.logical_and(zz == tall - 1, at < tall - 1)
        return jnp.logical_not(jnp.logical_or(low, high))

    def stores(s):
        slot = s % 2
        return [
            pltpu.make_async_copy(packed.at[slot], out_ref.at[me, s], store_sem.at[0, slot]),
            pltpu.make_async_copy(turned.at[slot], left_ref.at[s], store_sem.at[1, slot]),
        ]

    def normalize(s):
        slot = s % 2
        values = pool[ids_ref[s]].astype(jnp.float32)
        frames, width = values.shape
        center = values - jnp.sum(values, axis=0, keepdims=True) / frames
        spread = jnp.sum(center * center, axis=0, keepdims=True) / frames
        result = (center * (1.0 / jnp.sqrt(spread + 1e-05))).astype(jnp.bfloat16)
        turned[slot] = result.T
        tiles, top = width // LANES, frames // 2

        def pack(first, edge, upper, lower):
            for t in range(tiles):
                start = first + t * LANES
                packed[slot, t * frames : (t + 1) * frames, :] = result[:, start : start + LANES]
            ends = {upper: result[:top, edge : edge + HALF], lower: result[top:, edge : edge + HALF]}
            packed[slot, tiles * frames :, :] = jnp.concatenate([ends[0], ends[1]], axis=1)

        pl.when(c == 0)(lambda: pack(0, tiles * LANES, 0, 1))
        pl.when(c == 1)(lambda: pack(HALF, 0, 1, 0))

    def prepare(s, carry):
        @pl.when(s < total)
        def _():
            normalize(s)
            for copy_out in stores(s):
                copy_out.start()

        @pl.when(s >= 1)
        def _():
            for copy_out in stores(s - 1):
                copy_out.wait()
            for q in range(chunks):
                @pl.when(s == starts[q] + sizes[q])
                def _():
                    pl.when(has_up)(lambda: send(UP, me, q))
                    pl.when(has_down)(lambda: send(DOWN, me, q))
                    pl.when(by_side(z, z, q))(lambda: send(SIDE, me, q))
                    send(TWIN, me, q)

                if shares[q]:
                    ready = total if starts[q] == apart else held + starts[q] + shares[q]
                    pl.when(s == ready)(lambda: send(LATE, me, q))

        return carry

    load.wait()
    lax.fori_loop(0, total + 1, prepare, 0)

    def visit(k, q, act):
        pl.when(z - k >= 0)(lambda: act(device(z - k, x, c), q, "low", k))
        pl.when(z + k < tall)(lambda: act(device(z + k, x, c), q, "high", k))
        if q >= half:
            pl.when(jnp.logical_and(z - k == -1, has_down))(
                lambda: act(device(0, 1 - x, c), q, "bottom", k)
            )
            pl.when(jnp.logical_and(z + k == tall, has_up))(
                lambda: act(device(tall - 1, 1 - x, c), q, "top", k)
            )
        pl.when(k == 1)(lambda: act(device(z, 1 - x, c), q, "side", k))
        low = z - k + 1
        pl.when(jnp.logical_and(jnp.logical_and(k > 1, low >= 0), by_side(low, z, q)))(
            lambda: act(device(low, 1 - x, c), q, "end", k)
        )
        high = z + k - 1
        pl.when(jnp.logical_and(jnp.logical_and(k > 1, high < tall), by_side(high, z, q)))(
            lambda: act(device(high, 1 - x, c), q, "end", k)
        )

    def relay(block, q, kind, k):
        arrived(block, q)
        if kind == "low":
            pl.when(has_up)(lambda: send(UP, block, q))
            pl.when(by_side(z - k, z, q))(lambda: send(SIDE, block, q))
        if kind == "high":
            pl.when(has_down)(lambda: send(DOWN, block, q))
            pl.when(by_side(z + k, z, q))(lambda: send(SIDE, block, q))
        if kind == "bottom":
            pl.when(has_up)(lambda: send(UP, block, q))
        if kind == "top":
            pl.when(has_down)(lambda: send(DOWN, block, q))
        if kind == "side" and q >= half:
            pl.when(jnp.logical_and(z == 0, has_up))(lambda: send(UP, block, q))
            pl.when(jnp.logical_and(z == tall - 1, has_down))(lambda: send(DOWN, block, q))
        send(TWIN, block, q)
        if shares[q]:
            send(OVER, block, q)

    def pass_on(block, q, kind, k):
        copy(OVER, block, q).wait_recv()
        send(LATE, block, q)

    def step(k, carry):
        for q in range(chunks):
            pl.when(k <= tall)(lambda: visit(k, q, relay))
            if shares[q]:
                pl.when(k >= 2)(lambda: visit(k - 1, q, pass_on))
        return carry

    lax.fori_loop(1, tall + (2 if passed + split else 1), step, 0)

    def finish(zz, carry):
        for q in range(chunks):
            own = device(zz, x, c)
            other = device(zz, 1 - x, c)
            arrived(device(zz, x, 1 - c), q)
            arrived(device(zz, 1 - x, 1 - c), q)
            copy(TWIN, own, q).wait_send()
            copy(TWIN, other, q).wait_send()
            pl.when(by_side(zz, z, q))(lambda: copy(SIDE, own, q).wait_send())
            pl.when(jnp.logical_and(has_up, zz <= z))(lambda: copy(UP, own, q).wait_send())
            pl.when(jnp.logical_and(has_down, zz >= z))(lambda: copy(DOWN, own, q).wait_send())
            if q >= half:
                pl.when(jnp.logical_and(has_up, zz == 0))(
                    lambda: copy(UP, other, q).wait_send()
                )
                pl.when(jnp.logical_and(has_down, zz == tall - 1))(
                    lambda: copy(DOWN, other, q).wait_send()
                )
            if shares[q]:
                copy(LATE, device(zz, x, 1 - c), q).wait_recv()
                copy(LATE, device(zz, 1 - x, 1 - c), q).wait_recv()
                copy(LATE, own, q).wait_send()
                copy(LATE, other, q).wait_send()
                pl.when(zz != z)(lambda: copy(OVER, own, q).wait_send())
                copy(OVER, other, q).wait_send()
        return carry

    lax.fori_loop(0, tall, finish, 0)


def chunks_of(held, passed, split):
    late = held // 2
    rest = held - late - passed
    early_sizes = [1] * passed + [rest - rest // 2, rest // 2]
    late_sizes = [late - late // 3, late // 3]
    halves, start = [[], []], 0
    for half, sizes in zip(halves, [early_sizes, late_sizes]):
        for size in sizes:
            if size:
                half.append((start, size))
            start += size
    if split:
        halves[1].insert(0, (held + passed, 1))
    return halves


def gather(listed, series, count, subjects, form, collective_id):
    early, late = chunks_of(*form)
    pieces = early + late
    pool, frames, width = series.shape
    depth = width * frames // LANES
    return pl.pallas_call(
        functools.partial(gather_kernel, count, pieces, len(early), form),
        out_shape=[
            jax.ShapeDtypeStruct((count, subjects, depth, LANES), jnp.bfloat16),
            jax.ShapeDtypeStruct((subjects, width, frames), jnp.bfloat16),
        ],
        in_specs=[pl.BlockSpec(memory_space=pltpu.SMEM), pl.BlockSpec(memory_space=pl.ANY)],
        out_specs=[pl.BlockSpec(memory_space=pl.ANY)] * 2,
        scratch_shapes=[
            pltpu.VMEM((pool, frames, width), jnp.bfloat16),
            pltpu.VMEM((2, depth, LANES), jnp.bfloat16),
            pltpu.VMEM((2, width, frames), jnp.bfloat16),
            pltpu.SemaphoreType.DMA,
            pltpu.SemaphoreType.DMA((2, 2)),
            pltpu.SemaphoreType.DMA((6, count, len(pieces))),
            pltpu.SemaphoreType.DMA((2, count, len(pieces))),
        ],
        compiler_params=pltpu.CompilerParams(
            collective_id=collective_id, has_side_effects=True
        ),
        name="gather_{}_{}_{}".format(*form),
    )(listed, series)


def fisher_kernel(
    counts, labels_ref, me_ref, order_ref, matched_ref, number_ref, entry_ref,
    source_ref, blocks_ref, out_ref, left_ref, right, middle, zeros, done,
    zero_sem, done_sem, right_sem, left_sem,
):
    subjects, width, frames = left_ref.shape
    pairs = order_ref.shape[0] - 1
    own = labels_ref[me_ref[0]]
    tiles, top = width // LANES, frames // 2
    bound = LIMIT * frames
    strip = zeros.shape[0]
    matched = matched_ref[0]

    def columns(p):
        return pl.ds(pl.multiple_of(p * 2 * width, LANES), 2 * width)

    def blank(p, r):
        target = out_ref.at[r * strip : (r + 1) * strip, columns(p)]
        return pltpu.make_async_copy(zeros, target, zero_sem.at[p, r])

    def result(slot, p):
        return pltpu.make_async_copy(done.at[slot], out_ref.at[:, columns(p)], done_sem.at[slot])

    def empty(p):
        return jnp.logical_not(
            jnp.logical_or(labels_ref[2 * p] == own, labels_ref[2 * p + 1] == own)
        )

    def fetch(step, act):
        slot = step % 2
        for side in range(2):
            block = 2 * order_ref[step] + side

            @pl.when(labels_ref[block] == own)
            def _():
                act(
                    pltpu.make_async_copy(
                        blocks_ref.at[block], right.at[slot, side], right_sem.at[slot, side]
                    )
                )

    whole = pltpu.make_async_copy(source_ref, left_ref, left_sem)
    whole.start()
    fetch(0, lambda copy: copy.start())
    zeros[...] = jnp.zeros_like(zeros)

    def blanks(act):
        for p in range(pairs):
            @pl.when(empty(p))
            def _():
                for r in range(width // strip):
                    act(blank(p, r))

    def body(step, carry):
        spot = order_ref[step]
        first = labels_ref[2 * spot] == own
        second = labels_ref[2 * spot + 1] == own
        now = step % 2
        fetch(step, lambda copy: copy.wait())
        pl.when(step + 1 < matched)(lambda: fetch(step + 1, lambda copy: copy.start()))
        @pl.when(step == 0)
        def _():
            whole.wait()
            blanks(lambda copy: copy.start())

        pl.when(step >= 2)(lambda: result(now, spot).wait())

        for s in range(subjects):
            a = right[now, 0, s, tiles * frames :, :].astype(jnp.float32)
            b = right[now, 1, s, tiles * frames :, :].astype(jnp.float32)
            front = lax.broadcasted_iota(jnp.int32, a.shape, 1) < HALF
            middle[s, :top, :] = jnp.where(front, a, b).astype(jnp.bfloat16)
            swapped = pltpu.roll(jnp.where(front, b, a), HALF, 1)
            middle[s, top:, :] = swapped.astype(jnp.bfloat16)

        def tile(start, size, wanted, mixed, columns_of):
            lanes = pl.ds(start, size)

            def value(count):
                over = under = None
                for s in range(count):
                    slot = entry_ref[s]
                    these = columns_of(slot)
                    dot = jnp.dot(left_ref[slot], these, preferred_element_type=jnp.float32)
                    dot = jnp.clip(dot, -bound, bound)
                    plus, minus = frames + dot, frames - dot
                    if s < subjects - count:
                        plus, minus = plus * plus, minus * minus
                    over = plus if over is None else over * plus
                    under = minus if under is None else under * minus
                return 0.5 * jnp.log(over / under)

            @pl.when(jnp.logical_not(wanted))
            def _():
                done[now, :, lanes] = jnp.zeros((width, size), jnp.float32)

            for count in counts:
                @pl.when(jnp.logical_and(wanted, number_ref[0] == count))
                def _():
                    total = value(count)
                    if mixed:
                        lane = start + lax.broadcasted_iota(jnp.int32, total.shape, 1)
                        keep = jnp.where(
                            lane < width, first.astype(jnp.int32), second.astype(jnp.int32)
                        )
                        total = jnp.where(keep > 0, total, 0.0)
                    done[now, :, lanes] = total

        def stripe(side, slot, row):
            return right[now, side, slot, pl.ds(pl.multiple_of(row * frames, 16), frames), :]

        couples = tiles // 2
        spare = tiles % 2

        def couple(k, carry):
            side = k // couples
            row = 2 * (k % couples) + side * spare
            start = pl.multiple_of((side * (tiles + 1) + row) * LANES, LANES)
            tile(
                start, 2 * LANES, jnp.where(side == 0, first, second), False,
                lambda slot: jnp.concatenate(
                    [stripe(side, slot, row), stripe(side, slot, row + 1)], axis=1
                ),
            )
            return carry

        lax.fori_loop(0, 2 * couples, couple, 0)
        either = jnp.logical_or(first, second)
        if spare:
            tile(
                (tiles - 1) * LANES, 2 * LANES, either, True,
                lambda slot: jnp.concatenate([stripe(0, slot, tiles - 1), middle[slot]], axis=1),
            )
            tile((tiles + 1) * LANES, LANES, second, False, lambda slot: stripe(1, slot, 0))
        else:
            tile(tiles * LANES, LANES, either, True, lambda slot: middle[slot])

        result(now, spot).start()
        return carry

    lax.fori_loop(0, matched, body, 0)
    final = matched - 1
    result(final % 2, order_ref[final]).wait()

    @pl.when(final >= 1)
    def _():
        result((final - 1) % 2, order_ref[jnp.maximum(final - 1, 0)]).wait()

    blanks(lambda copy: copy.wait())


def correlate(left, blocks, labels, me, table):
    order, matched, number, entry = table
    count, subjects, depth, _ = blocks.shape
    _, width, frames = left.shape
    strips = 8 if width % 64 == 0 else 1
    smem = pl.BlockSpec(memory_space=pltpu.SMEM)
    hbm = pl.BlockSpec(memory_space=pl.ANY)
    return pl.pallas_call(
        functools.partial(fisher_kernel, [subjects - again for again in range(SQUARES + 1)]),
        in_specs=[smem] * 6 + [hbm, hbm],
        out_specs=hbm,
        scratch_shapes=[
            pltpu.VMEM((subjects, width, frames), jnp.bfloat16),
            pltpu.VMEM((2, 2, subjects, depth, LANES), jnp.bfloat16),
            pltpu.VMEM((subjects, frames, LANES), jnp.bfloat16),
            pltpu.VMEM((width // strips, 2 * width), jnp.float32),
            pltpu.VMEM((2, width, 2 * width), jnp.float32),
            pltpu.SemaphoreType.DMA((count // 2, strips)),
            pltpu.SemaphoreType.DMA((2,)),
            pltpu.SemaphoreType.DMA((2, 2)),
            pltpu.SemaphoreType.DMA,
        ],
        out_shape=jax.ShapeDtypeStruct((width, count * width), jnp.float32),
        compiler_params=pltpu.CompilerParams(
            vmem_limit_bytes=60 * 1024 * 1024
        ),
        name="correlate",
    )(labels, me, order, matched, number, entry, left, blocks)


def on_device(series, subject_ids, net_labels):
    count = lax.axis_size("blk")
    pool, frames, width = series.shape
    subjects = subject_ids.shape[0]
    packs = width % LANES == HALF and frames % 32 == 0 and width * frames // LANES % 32 == 0
    fits = net_labels.shape[0] == count and count % 4 == 0 and lax.axis_size("parts") == 2
    if not (packs and fits and pool < 32 and subjects == FORMS[-1][0]):
        return plain(series, subject_ids, net_labels)
    me = lax.axis_index("blk").astype(jnp.int32)[None]
    part = lax.axis_index("parts").astype(jnp.int32)[None]
    others = lax.ppermute(subject_ids, "parts", [(0, 1), (1, 0)])
    listed, chosen, *table = distinct(pool, subject_ids, others, part, net_labels, me)
    runs = [
        functools.partial(gather, count=count, subjects=subjects, form=form, collective_id=i)
        for i, form in enumerate(FORMS)
    ]
    blocks, left = lax.switch(chosen[0], runs, listed, series)
    return correlate(left, blocks, net_labels, me, table)


def solution(mesh):
    return jax.shard_map(
        on_device,
        mesh=mesh,
        in_specs=(P(None, None, "blk"), P("parts"), P()),
        out_specs=P(("parts", "blk"), None),
        check_vma=False,
    )
```

```python
import functools

import jax
import jax.numpy as jnp
from jax import lax
from jax.experimental import pallas as pl
from jax.experimental.pallas import tpu as pltpu
from jax.sharding import PartitionSpec as P

LIMIT = 0.999
LANES = 128
HALF = LANES // 2
SQUARES = 3
FORMS = [(4, 1, 1), (4, 2, 0), (5, 2, 0), (5, 2, 1), (6, 2, 0), (8, 0, 0)]


def normalize(chosen):
    values = chosen.astype(jnp.float32)
    center = values - jnp.mean(values, axis=1, keepdims=True)
    spread = jnp.mean(center * center, axis=1, keepdims=True)
    return (center / jnp.sqrt(spread + 1e-05)).astype(jnp.bfloat16)


def fisher_sum(left, right):
    frames = left.shape[1]
    total = jnp.zeros((left.shape[2], right.shape[2]), jnp.float32)
    for subject in range(left.shape[0]):
        corr = (
            lax.dot_general(
                left[subject],
                right[subject],
                (((0,), (0,)), ((), ())),
                preferred_element_type=jnp.float32,
            )
            / frames
        )
        clipped = jnp.clip(corr, -LIMIT, LIMIT)
        total = total + 0.5 * jnp.log((1.0 + clipped) / (1.0 - clipped))
    return total


def plain(series, subject_ids, net_labels):
    normalized = normalize(jnp.take(series, subject_ids, axis=0))
    rows = normalized.shape[2]
    index = lax.axis_index("blk")
    count = lax.axis_size("blk")
    row_labels = jnp.repeat(net_labels, count * rows // net_labels.shape[0])
    own_labels = lax.dynamic_slice_in_dim(row_labels, index * rows, rows)
    gathered = lax.all_gather(normalized, "blk", axis=2, tiled=True)
    same = own_labels[:, None] == row_labels[None, :]
    return jnp.where(same, fisher_sum(normalized, gathered), 0.0)


def plan_kernel(
    pool, mine_ref, theirs_ref, first_ref, labels_ref, me_ref,
    list_ref, form_ref, order_ref, pairs_ref, number_ref, entry_ref,
    where_ref, pair_ref,
):
    subjects = mine_ref.shape[0]
    one, zero = jnp.int32(1), jnp.int32(0)

    def members(ref):
        bits = zero
        for s in range(subjects):
            bits = bits | (one << ref[s])
        return [(bits >> p) & 1 for p in range(pool)]

    mine, theirs = members(mine_ref), members(theirs_ref)
    own, other = sum(mine), sum(theirs)
    both = sum(a * b for a, b in zip(mine, theirs))
    form = jnp.int32(len(FORMS) - 1)
    held, late, split = (jnp.int32(value) for value in FORMS[-1])
    for index in reversed(range(len(FORMS) - 1)):
        carried, passed, halved = FORMS[index]
        lack = jnp.maximum(own - halved - carried, 0)
        give = jnp.maximum(other - halved - carried, 0)
        fits = jnp.logical_and(jnp.maximum(lack, give) <= passed, lack + give + halved <= both)
        form = jnp.where(fits, index, form)
        held = jnp.where(fits, carried, held)
        late = jnp.where(fits, passed, late)
        split = jnp.where(fits, halved, split)
    form_ref[0] = form
    lack, give = jnp.maximum(own - split - held, 0), jnp.maximum(other - split - held, 0)
    first = first_ref[0] == 0
    give_from = jnp.where(first, 0, lack)
    lack_from = jnp.where(first, give, 0)
    for s in range(list_ref.shape[0]):
        list_ref[s] = mine_ref[0]
    rank, plain_at = zero, give
    for p in range(pool):
        common = mine[p] * theirs[p]
        gives = jnp.logical_and(rank >= give_from, rank < give_from + give)
        gives = jnp.logical_and(gives, common == 1)
        lacks = jnp.logical_and(rank >= lack_from, rank < lack_from + lack)
        lacks = jnp.logical_and(lacks, common == 1)
        halves = jnp.logical_and(common * split == 1, rank == lack + give)
        at = jnp.where(gives, rank - give_from, jnp.where(lacks, held + rank - lack_from, plain_at))
        at = jnp.where(halves, held + late, at)
        moved = jnp.logical_or(halves, jnp.logical_or(gives, lacks))
        kept = jnp.logical_and(mine[p] == 1, jnp.logical_not(moved))
        plain_at = plain_at + kept.astype(jnp.int32)
        rank = rank + common
        where_ref[p] = at
        list_ref[jnp.where(mine[p] == 1, at, subjects)] = jnp.int32(p)
    ids = [mine_ref[s] for s in range(subjects)]
    doubles, singles, taken = [], [], zero
    for s in range(subjects):
        same = [(ids[r] == ids[s]).astype(jnp.int32) for r in range(subjects)]
        before, times = sum(same[:s], zero), sum(same)
        opens = before % 2 == 0
        double = jnp.logical_and(opens, times > before + 1)
        double = jnp.logical_and(double, taken < SQUARES).astype(jnp.int32)
        taken = taken + double
        closes = jnp.where(opens, 0, pair_ref[ids[s]])
        pair_ref[ids[s]] = double
        doubles.append(double)
        singles.append(1 - double - closes)
    number_ref[0] = subjects - taken
    many_at, one_at = zero, taken
    for s in range(subjects):
        at = jnp.where(doubles[s] == 1, many_at, jnp.where(singles[s] == 1, one_at, subjects))
        entry_ref[at] = where_ref[ids[s]]
        many_at, one_at = many_at + doubles[s], one_at + singles[s]

    label = labels_ref[me_ref[0]]
    pairs = order_ref.shape[0] - 1
    found = zero
    for p in range(pairs):
        front, back = labels_ref[2 * p] == label, labels_ref[2 * p + 1] == label
        hit = jnp.logical_or(front, back)
        at = jnp.where(hit, found, pairs)
        order_ref[at] = jnp.int32(p)
        found = found + hit.astype(jnp.int32)
    pairs_ref[0] = found


def distinct(pool, mine, theirs, part, labels, me):
    subjects = mine.shape[0]
    spots = labels.shape[0] // 2 + 1
    sizes = [subjects + 1, 1, spots, 1, 1, subjects + 1]
    return pl.pallas_call(
        functools.partial(plan_kernel, pool),
        out_shape=[jax.ShapeDtypeStruct((size,), jnp.int32) for size in sizes],
        in_specs=[pl.BlockSpec(memory_space=pltpu.SMEM)] * 5,
        out_specs=[pl.BlockSpec(memory_space=pltpu.SMEM)] * len(sizes),
        scratch_shapes=[pltpu.SMEM((pool,), jnp.int32)] * 2,
        name="plan",
    )(mine, theirs, part, labels, me)


def gather_kernel(
    count, pieces, half, form, ids_ref, series_ref, out_ref, left_ref,
    pool, packed, turned, load_sem, store_sem, send_sem, recv_sem,
):
    tall = count // 4
    me = lax.axis_index("blk")
    part = lax.axis_index("parts")
    z = me // 4
    x = (me // 2) % 2
    c = me % 2
    held, passed, split = form
    chunks = len(pieces)
    starts = [start for start, _ in pieces]
    sizes = [size for _, size in pieces]
    apart = held + passed
    total = apart + split
    shares = [
        1 if start == apart and split else max(0, min(passed - start, size))
        for start, size in pieces
    ]
    rows = out_ref.shape[2] // 2
    near = pl.ds(pl.multiple_of(part * rows, 16), rows)
    far = pl.ds(pl.multiple_of((1 - part) * rows, 16), rows)
    UP, DOWN, SIDE, TWIN, OVER, LATE = range(6)

    def device(zz, xx, cc):
        return (zz * 2 + xx) * 2 + cc

    target = {
        UP: {"blk": device(jnp.minimum(z + 1, tall - 1), x, c)},
        DOWN: {"blk": device(jnp.maximum(z - 1, 0), x, c)},
        SIDE: {"blk": device(z, 1 - x, c)},
        TWIN: {"blk": device(z, x, 1 - c)},
        OVER: {"parts": 1 - part},
        LATE: {"blk": device(z, x, 1 - c)},
    }
    has_up, has_down = z + 1 < tall, z > 0

    load = pltpu.make_async_copy(series_ref, pool, load_sem)
    load.start()
    barrier = pltpu.get_barrier_semaphore()

    def greet(way):
        pl.semaphore_signal(
            barrier, inc=1, device_id=target[way], device_id_type=pl.DeviceIdType.MESH
        )

    greet(SIDE)
    greet(TWIN)
    greet(OVER)
    pl.when(has_up)(lambda: greet(UP))
    pl.when(has_down)(lambda: greet(DOWN))
    pl.semaphore_wait(barrier, 3 + has_up.astype(jnp.int32) + has_down.astype(jnp.int32))

    def copy(way, block, q):
        late = int(way in (OVER, LATE))
        if split and starts[q] == apart:
            source = landing = (block, apart, far if way == LATE else near)
        elif late:
            landing = (block, pl.ds(held + starts[q], shares[q]))
            source = landing if way == LATE else (block, pl.ds(starts[q], shares[q]))
        else:
            source = landing = (block, pl.ds(starts[q], sizes[q]))
        return pltpu.make_async_remote_copy(
            src_ref=out_ref.at[source],
            dst_ref=out_ref.at[landing],
            send_sem=send_sem.at[way, block, q],
            recv_sem=recv_sem.at[late, block, q],
            device_id=target[way],
            device_id_type=pl.DeviceIdType.MESH,
        )

    def send(way, block, q):
        copy(way, block, q).start()

    def arrived(block, q):
        copy(TWIN, block, q).wait_recv()

    def by_side(zz, at, q):
        if q < half:
            return jnp.bool_(True)
        low = jnp.logical_and(zz == 0, at > 0)
        high = jnp.logical_and(zz == tall - 1, at < tall - 1)
        return jnp.logical_not(jnp.logical_or(low, high))

    def stores(s):
        slot = s % 2
        return [
            pltpu.make_async_copy(packed.at[slot], out_ref.at[me, s], store_sem.at[0, slot]),
            pltpu.make_async_copy(turned.at[slot], left_ref.at[s], store_sem.at[1, slot]),
        ]

    def normalize(s):
        slot = s % 2
        values = pool[ids_ref[s]].astype(jnp.float32)
        frames, width = values.shape
        center = values - jnp.sum(values, axis=0, keepdims=True) / frames
        spread = jnp.sum(center * center, axis=0, keepdims=True) / frames
        result = (center * (1.0 / jnp.sqrt(spread + 1e-05))).astype(jnp.bfloat16)
        turned[slot] = result.T
        tiles, top = width // LANES, frames // 2

        def pack(first, edge, upper, lower):
            for t in range(tiles):
                start = first + t * LANES
                packed[slot, t * frames : (t + 1) * frames, :] = result[:, start : start + LANES]
            ends = {upper: result[:top, edge : edge + HALF], lower: result[top:, edge : edge + HALF]}
            packed[slot, tiles * frames :, :] = jnp.concatenate([ends[0], ends[1]], axis=1)

        pl.when(c == 0)(lambda: pack(0, tiles * LANES, 0, 1))
        pl.when(c == 1)(lambda: pack(HALF, 0, 1, 0))

    def prepare(s, carry):
        @pl.when(s >= 1)
        def _():
            for copy_out in stores(s - 1):
                copy_out.wait()
            for q in range(chunks):
                @pl.when(s == starts[q] + sizes[q])
                def _():
                    pl.when(has_up)(lambda: send(UP, me, q))
                    pl.when(has_down)(lambda: send(DOWN, me, q))
                    pl.when(by_side(z, z, q))(lambda: send(SIDE, me, q))
                    send(TWIN, me, q)

                if shares[q]:
                    ready = total if starts[q] == apart else held + starts[q] + shares[q]
                    pl.when(s == ready)(lambda: send(LATE, me, q))

        @pl.when(s < total)
        def _():
            normalize(s)
            for copy_out in stores(s):
                copy_out.start()

        return carry

    load.wait()
    lax.fori_loop(0, total + 1, prepare, 0)

    def visit(k, q, act):
        pl.when(z - k >= 0)(lambda: act(device(z - k, x, c), q, "low", k))
        pl.when(z + k < tall)(lambda: act(device(z + k, x, c), q, "high", k))
        if q >= half:
            pl.when(jnp.logical_and(z - k == -1, has_down))(
                lambda: act(device(0, 1 - x, c), q, "bottom", k)
            )
            pl.when(jnp.logical_and(z + k == tall, has_up))(
                lambda: act(device(tall - 1, 1 - x, c), q, "top", k)
            )
        pl.when(k == 1)(lambda: act(device(z, 1 - x, c), q, "side", k))
        low = z - k + 1
        pl.when(jnp.logical_and(jnp.logical_and(k > 1, low >= 0), by_side(low, z, q)))(
            lambda: act(device(low, 1 - x, c), q, "end", k)
        )
        high = z + k - 1
        pl.when(jnp.logical_and(jnp.logical_and(k > 1, high < tall), by_side(high, z, q)))(
            lambda: act(device(high, 1 - x, c), q, "end", k)
        )

    def relay(block, q, kind, k):
        arrived(block, q)
        if kind == "low":
            pl.when(has_up)(lambda: send(UP, block, q))
            pl.when(by_side(z - k, z, q))(lambda: send(SIDE, block, q))
        if kind == "high":
            pl.when(has_down)(lambda: send(DOWN, block, q))
            pl.when(by_side(z + k, z, q))(lambda: send(SIDE, block, q))
        if kind == "bottom":
            pl.when(has_up)(lambda: send(UP, block, q))
        if kind == "top":
            pl.when(has_down)(lambda: send(DOWN, block, q))
        if kind == "side" and q >= half:
            pl.when(jnp.logical_and(z == 0, has_up))(lambda: send(UP, block, q))
            pl.when(jnp.logical_and(z == tall - 1, has_down))(lambda: send(DOWN, block, q))
        send(TWIN, block, q)
        if shares[q]:
            send(OVER, block, q)

    def pass_on(block, q, kind, k):
        copy(OVER, block, q).wait_recv()
        send(LATE, block, q)

    def step(k, carry):
        for q in range(chunks):
            pl.when(k <= tall)(lambda: visit(k, q, relay))
            if shares[q]:
                pl.when(k >= 2)(lambda: visit(k - 1, q, pass_on))
        return carry

    lax.fori_loop(1, tall + (2 if passed + split else 1), step, 0)

    def finish(zz, carry):
        for q in range(chunks):
            own = device(zz, x, c)
            other = device(zz, 1 - x, c)
            arrived(device(zz, x, 1 - c), q)
            arrived(device(zz, 1 - x, 1 - c), q)
            copy(TWIN, own, q).wait_send()
            copy(TWIN, other, q).wait_send()
            pl.when(by_side(zz, z, q))(lambda: copy(SIDE, own, q).wait_send())
            pl.when(jnp.logical_and(has_up, zz <= z))(lambda: copy(UP, own, q).wait_send())
            pl.when(jnp.logical_and(has_down, zz >= z))(lambda: copy(DOWN, own, q).wait_send())
            if q >= half:
                pl.when(jnp.logical_and(has_up, zz == 0))(
                    lambda: copy(UP, other, q).wait_send()
                )
                pl.when(jnp.logical_and(has_down, zz == tall - 1))(
                    lambda: copy(DOWN, other, q).wait_send()
                )
            if shares[q]:
                copy(LATE, device(zz, x, 1 - c), q).wait_recv()
                copy(LATE, device(zz, 1 - x, 1 - c), q).wait_recv()
                copy(LATE, own, q).wait_send()
                copy(LATE, other, q).wait_send()
                pl.when(zz != z)(lambda: copy(OVER, own, q).wait_send())
                copy(OVER, other, q).wait_send()
        return carry

    lax.fori_loop(0, tall, finish, 0)


def chunks_of(held, passed, split):
    late = held // 2
    rest = held - late - passed
    early_sizes = [1] * passed + [rest - rest // 2, rest // 2]
    late_sizes = [late - late // 3, late // 3]
    halves, start = [[], []], 0
    for half, sizes in zip(halves, [early_sizes, late_sizes]):
        for size in sizes:
            if size:
                half.append((start, size))
            start += size
    if split:
        halves[1].insert(0, (held + passed, 1))
    return halves


def gather(listed, series, count, subjects, form, collective_id):
    early, late = chunks_of(*form)
    pieces = early + late
    pool, frames, width = series.shape
    depth = width * frames // LANES
    return pl.pallas_call(
        functools.partial(gather_kernel, count, pieces, len(early), form),
        out_shape=[
            jax.ShapeDtypeStruct((count, subjects, depth, LANES), jnp.bfloat16),
            jax.ShapeDtypeStruct((subjects, width, frames), jnp.bfloat16),
        ],
        in_specs=[pl.BlockSpec(memory_space=pltpu.SMEM), pl.BlockSpec(memory_space=pl.ANY)],
        out_specs=[pl.BlockSpec(memory_space=pl.ANY)] * 2,
        scratch_shapes=[
            pltpu.VMEM((pool, frames, width), jnp.bfloat16),
            pltpu.VMEM((2, depth, LANES), jnp.bfloat16),
            pltpu.VMEM((2, width, frames), jnp.bfloat16),
            pltpu.SemaphoreType.DMA,
            pltpu.SemaphoreType.DMA((2, 2)),
            pltpu.SemaphoreType.DMA((6, count, len(pieces))),
            pltpu.SemaphoreType.DMA((2, count, len(pieces))),
        ],
        compiler_params=pltpu.CompilerParams(
            collective_id=collective_id, has_side_effects=True
        ),
        name="gather_{}_{}_{}".format(*form),
    )(listed, series)


def fisher_kernel(
    counts, labels_ref, me_ref, order_ref, matched_ref, number_ref, entry_ref,
    source_ref, blocks_ref, out_ref, left_ref, right, middle, zeros, done,
    zero_sem, done_sem, right_sem, left_sem,
):
    subjects, width, frames = left_ref.shape
    pairs = order_ref.shape[0] - 1
    own = labels_ref[me_ref[0]]
    tiles, top = width // LANES, frames // 2
    bound = LIMIT * frames
    strip = zeros.shape[0]
    matched = matched_ref[0]

    def columns(p):
        return pl.ds(pl.multiple_of(p * 2 * width, LANES), 2 * width)

    def blank(p, r):
        target = out_ref.at[r * strip : (r + 1) * strip, columns(p)]
        return pltpu.make_async_copy(zeros, target, zero_sem.at[p, r])

    def result(slot, p):
        return pltpu.make_async_copy(done.at[slot], out_ref.at[:, columns(p)], done_sem.at[slot])

    def empty(p):
        return jnp.logical_not(
            jnp.logical_or(labels_ref[2 * p] == own, labels_ref[2 * p + 1] == own)
        )

    def fetch(step, act):
        slot = step % 2
        for side in range(2):
            block = 2 * order_ref[step] + side

            @pl.when(labels_ref[block] == own)
            def _():
                act(
                    pltpu.make_async_copy(
                        blocks_ref.at[block], right.at[slot, side], right_sem.at[slot, side]
                    )
                )

    whole = pltpu.make_async_copy(source_ref, left_ref, left_sem)
    whole.start()
    fetch(0, lambda copy: copy.start())
    zeros[...] = jnp.zeros_like(zeros)

    def blanks(act):
        for p in range(pairs):
            @pl.when(empty(p))
            def _():
                for r in range(width // strip):
                    act(blank(p, r))

    def body(step, carry):
        spot = order_ref[step]
        first = labels_ref[2 * spot] == own
        second = labels_ref[2 * spot + 1] == own
        now = step % 2
        fetch(step, lambda copy: copy.wait())
        pl.when(step + 1 < matched)(lambda: fetch(step + 1, lambda copy: copy.start()))
        @pl.when(step == 0)
        def _():
            whole.wait()
            blanks(lambda copy: copy.start())

        pl.when(step >= 2)(lambda: result(now, spot).wait())

        for s in range(subjects):
            a = right[now, 0, s, tiles * frames :, :].astype(jnp.float32)
            b = right[now, 1, s, tiles * frames :, :].astype(jnp.float32)
            front = lax.broadcasted_iota(jnp.int32, a.shape, 1) < HALF
            middle[s, :top, :] = jnp.where(front, a, b).astype(jnp.bfloat16)
            swapped = pltpu.roll(jnp.where(front, b, a), HALF, 1)
            middle[s, top:, :] = swapped.astype(jnp.bfloat16)

        def tile(start, size, wanted, mixed, columns_of):
            lanes = pl.ds(start, size)

            def value(count):
                over = under = None
                for s in range(count):
                    slot = entry_ref[s]
                    these = columns_of(slot)
                    dot = jnp.dot(left_ref[slot], these, preferred_element_type=jnp.float32)
                    dot = jnp.clip(dot, -bound, bound)
                    plus, minus = frames + dot, frames - dot
                    if s < subjects - count:
                        plus, minus = plus * plus, minus * minus
                    over = plus if over is None else over * plus
                    under = minus if under is None else under * minus
                return 0.5 * jnp.log(over / under)

            @pl.when(jnp.logical_not(wanted))
            def _():
                done[now, :, lanes] = jnp.zeros((width, size), jnp.float32)

            for count in counts:
                @pl.when(jnp.logical_and(wanted, number_ref[0] == count))
                def _():
                    total = value(count)
                    if mixed:
                        lane = start + lax.broadcasted_iota(jnp.int32, total.shape, 1)
                        keep = jnp.where(
                            lane < width, first.astype(jnp.int32), second.astype(jnp.int32)
                        )
                        total = jnp.where(keep > 0, total, 0.0)
                    done[now, :, lanes] = total

        def stripe(side, slot, row):
            return right[now, side, slot, pl.ds(pl.multiple_of(row * frames, 16), frames), :]

        couples = tiles // 2
        spare = tiles % 2

        def couple(k, carry):
            side = k // couples
            row = 2 * (k % couples) + side * spare
            start = pl.multiple_of((side * (tiles + 1) + row) * LANES, LANES)
            tile(
                start, 2 * LANES, jnp.where(side == 0, first, second), False,
                lambda slot: jnp.concatenate(
                    [stripe(side, slot, row), stripe(side, slot, row + 1)], axis=1
                ),
            )
            return carry

        lax.fori_loop(0, 2 * couples, couple, 0)
        either = jnp.logical_or(first, second)
        if spare:
            tile(
                (tiles - 1) * LANES, 2 * LANES, either, True,
                lambda slot: jnp.concatenate([stripe(0, slot, tiles - 1), middle[slot]], axis=1),
            )
            tile((tiles + 1) * LANES, LANES, second, False, lambda slot: stripe(1, slot, 0))
        else:
            tile(tiles * LANES, LANES, either, True, lambda slot: middle[slot])

        result(now, spot).start()
        return carry

    lax.fori_loop(0, matched, body, 0)
    final = matched - 1
    result(final % 2, order_ref[final]).wait()

    @pl.when(final >= 1)
    def _():
        result((final - 1) % 2, order_ref[jnp.maximum(final - 1, 0)]).wait()

    blanks(lambda copy: copy.wait())


def correlate(left, blocks, labels, me, table):
    order, matched, number, entry = table
    count, subjects, depth, _ = blocks.shape
    _, width, frames = left.shape
    strips = 8 if width % 64 == 0 else 1
    smem = pl.BlockSpec(memory_space=pltpu.SMEM)
    hbm = pl.BlockSpec(memory_space=pl.ANY)
    return pl.pallas_call(
        functools.partial(fisher_kernel, [subjects - again for again in range(SQUARES + 1)]),
        in_specs=[smem] * 6 + [hbm, hbm],
        out_specs=hbm,
        scratch_shapes=[
            pltpu.VMEM((subjects, width, frames), jnp.bfloat16),
            pltpu.VMEM((2, 2, subjects, depth, LANES), jnp.bfloat16),
            pltpu.VMEM((subjects, frames, LANES), jnp.bfloat16),
            pltpu.VMEM((width // strips, 2 * width), jnp.float32),
            pltpu.VMEM((2, width, 2 * width), jnp.float32),
            pltpu.SemaphoreType.DMA((count // 2, strips)),
            pltpu.SemaphoreType.DMA((2,)),
            pltpu.SemaphoreType.DMA((2, 2)),
            pltpu.SemaphoreType.DMA,
        ],
        out_shape=jax.ShapeDtypeStruct((width, count * width), jnp.float32),
        compiler_params=pltpu.CompilerParams(
            vmem_limit_bytes=60 * 1024 * 1024
        ),
        name="correlate",
    )(labels, me, order, matched, number, entry, left, blocks)


def on_device(series, subject_ids, net_labels):
    count = lax.axis_size("blk")
    pool, frames, width = series.shape
    subjects = subject_ids.shape[0]
    packs = width % LANES == HALF and frames % 32 == 0 and width * frames // LANES % 32 == 0
    fits = net_labels.shape[0] == count and count % 4 == 0 and lax.axis_size("parts") == 2
    if not (packs and fits and pool < 32 and subjects == FORMS[-1][0]):
        return plain(series, subject_ids, net_labels)
    me = lax.axis_index("blk").astype(jnp.int32)[None]
    part = lax.axis_index("parts").astype(jnp.int32)[None]
    others = lax.ppermute(subject_ids, "parts", [(0, 1), (1, 0)])
    listed, chosen, *table = distinct(pool, subject_ids, others, part, net_labels, me)
    runs = [
        functools.partial(gather, count=count, subjects=subjects, form=form, collective_id=i)
        for i, form in enumerate(FORMS)
    ]
    blocks, left = lax.switch(chosen[0], runs, listed, series)
    return correlate(left, blocks, net_labels, me, table)


def solution(mesh):
    return jax.shard_map(
        on_device,
        mesh=mesh,
        in_specs=(P(None, None, "blk"), P("parts"), P()),
        out_specs=P(("parts", "blk"), None),
        check_vma=False,
    )
```
